512 devices in a mesh: seq: 64 (over y, z), head: 8 (over x, core).
Axes of the slice: x: 4, y: 4, z: 16, core: 2. Of those that a mesh axis runs over, the one named last changes fastest.
Arguments:
- features: bfloat16 [32768, 2048], P('seq', 'head'), may hold values from -6 to 6
- gate_weight: bfloat16 [2048, 16], P('head'), may hold values from -0.125 to 0.125
- queries: bfloat16 [32768, 2048], P('seq', 'head'), may hold values from -6 to 6
- keys: bfloat16 [32768, 2048], P('seq', 'head'), may hold values from -40 to 40, as said below
- values: bfloat16 [32768, 2048], P('seq', 'head'), may hold values from -6 to 6
- log_decay: float32 [32768, 16], P('seq', 'head'), may hold values from -1.5 to 0, as said below
- ridge: float32 [16, 128], P('head'), may hold values from 0.02 to 0.5
Outputs:
- mixed: bfloat16 [32768, 2048], P('seq', 'head')
The draws below stay inside these ranges and needn't reach their ends.
Inputs may be any that keep to these rules, and one draw needn't show every extreme that they name: `keys`: keys are real-valued of order one to ten in size. `log_decay`: each entry is at most zero.
All inputs are finite; a program needn't handle non-finite values.
Results may differ from the reference program's by a relative error of at most 0.001.
Values may be sent and summed in bfloat16 or wider, within the bound.
A program may use at most 64 MiB of HBM per device.

```python
import math
import jax
import jax.numpy as jnp
from jax import lax

D = 2048
HD = 128
TOK_DEV = 512
GROUP = 128
CG_STEPS = 4
H = 16
TOKENS = 32768


def draw_keys(key, part):
    base_key, scale_key = jax.random.split(key, 2)
    scales = jnp.exp(jax.random.uniform(scale_key, (H * HD,), jnp.float32, 0.0, math.log(10.0)))
    base = jnp.clip(jax.random.normal(base_key, (TOKENS, H * HD), jnp.float32), -4.0, 4.0)
    return (base * scales[None, :]).astype(jnp.bfloat16)


def draw_log_decay(key, part):
    keyset = jax.random.split(key, 7)
    pick = jax.random.uniform(keyset[0], (H,), jnp.float32)
    slow = pick < 0.5
    slow_rate = jnp.exp(jax.random.uniform(keyset[1], (H,), jnp.float32, math.log(0.2 / TOKENS), math.log(0.8 / TOKENS)))
    fast_rate = jnp.exp(jax.random.uniform(keyset[2], (H,), jnp.float32, math.log(1.0 / 50.0), math.log(1.0 / 30.0)))
    decay_speed = jnp.where(slow, slow_rate, fast_rate)
    random_noise = jax.random.uniform(keyset[3], (TOKENS, H), jnp.float32, 0.5, 1.5)
    shard_factor = jax.random.uniform(keyset[4], (TOKENS // TOK_DEV, 1, H), jnp.float32, 0.5, 2.0)
    partition_whole = jnp.broadcast_to(shard_factor, (TOKENS // TOK_DEV, TOK_DEV, H)).reshape(TOKENS, H)
    places = jax.random.randint(keyset[5], (2, H), 0, TOKENS)
    loss_values = jax.random.uniform(keyset[6], (2, H), jnp.float32, 0.2, 0.4)
    position = jnp.arange(TOKENS, dtype=jnp.int32)
    stricken_rows = position[:, None, None] == places[None, :, :]
    spike_amount = jnp.sum(jnp.where(stricken_rows, -jnp.log(1.0 - loss_values)[None, :, :], 0.0), axis=1)
    return -(decay_speed[None, :] * random_noise * partition_whole) - spike_amount


def shard_levels(own_key, shape, cuts, least, top_value):
    level = 1.0
    for dim, parts in cuts:
        steps = jax.random.uniform(jax.random.fold_in(jax.random.fold_in(own_key, 6), dim), (parts,), jnp.float32, least / len(cuts), top_value / len(cuts))
        level = level * jnp.repeat(jnp.exp(steps), shape[dim] // parts).reshape((-1,) + (1,) * (len(shape) - 1 - dim))
    return level


def scatter_about(rng, extent, scale, most, cuts=(), held_as=jnp.bfloat16):
    entries = jax.random.normal(rng, extent, jnp.float32) * scale
    if len(cuts) > 0:
        entries = shard_levels(rng, extent, cuts, -0.22, 0.18) * entries
    return jnp.clip(entries, min=-most, max=most).astype(held_as)


def setup_inputs(seed: int = 0) -> dict:
    splits = jax.random.split(jax.random.key(seed), 8)
    features = scatter_about(splits[0], (TOKENS, D), 1.0, 6.0, ((0, 64), (1, 8)))
    gate_weight = scatter_about(splits[1], (D, H), D ** -0.5, 0.125, ((0, 8),))
    queries = scatter_about(splits[2], (TOKENS, H * HD), 1.0, 6.0, ((0, 64), (1, 8)))
    keys = draw_keys(jax.random.fold_in(splits[7], 71), 0)
    values = scatter_about(splits[4], (TOKENS, H * HD), 1.0, 6.0, ((0, 64), (1, 8)))
    log_decay = draw_log_decay(jax.random.fold_in(splits[7], 71), 0)
    ridge = jnp.clip(jnp.exp(math.log(0.5) - 3.218876 * jax.random.uniform(splits[6], (H, HD), jnp.float32) ** shard_levels(splits[6], (H, HD), ((0, 8),), -0.2, 0.2)), 0.02, 0.5)
    return {"features": features, "gate_weight": gate_weight, "queries": queries, "keys": keys, "values": values, "log_decay": log_decay, "ridge": ridge}


HIGH = lax.Precision.HIGHEST

def unit_rows(block):
    return block / jnp.sqrt(lax.optimization_barrier(jnp.sum(block * block, axis=-1, keepdims=True)) + 1e-06)

def head_pass(packed):
    query_all, key_all, value_all, decay_all, beta_all, ridge_row = packed
    block_groups = TOKENS // GROUP
    query_blocks = unit_rows(query_all).reshape(block_groups, GROUP, HD)
    key_blocks = unit_rows(key_all).reshape(block_groups, GROUP, HD)
    value_blocks = value_all.reshape(block_groups, GROUP, HD)
    decay_blocks = decay_all.reshape(block_groups, GROUP)
    beta_blocks = beta_all.reshape(block_groups, GROUP)
    lower = jnp.tril(jnp.ones((GROUP, GROUP), dtype=bool))

    def one_block(carry, item):
        state_kk, state_vk = carry
        query_c, key_c, value_c, decay_c, beta_c = item
        within = jnp.cumsum(decay_c)
        spread = within[:, None] - within[None, :]
        weights = jnp.where(lower, jnp.exp(jnp.where(lower, spread, 0.0)), 0.0) * beta_c[None, :]
        lead = jnp.exp(within)[:, None]

        def apply_op(vecs):
            inner = jnp.dot(vecs, state_kk.T, precision=HIGH)
            scores = jnp.dot(vecs, key_c.T, precision=HIGH) * weights
            return lead * inner + jnp.dot(scores, key_c, precision=HIGH) + ridge_row[None, :] * vecs
        solution = jnp.zeros_like(query_c)
        resid = query_c
        direction = query_c
        norm_now = lax.optimization_barrier(jnp.sum(resid * resid, axis=-1, keepdims=True))
        for step in range(CG_STEPS):
            image = apply_op(direction)
            alpha = norm_now / lax.optimization_barrier(jnp.sum(direction * image, axis=-1, keepdims=True))
            solution = solution + alpha * direction
            resid = resid - alpha * image
            norm_next = lax.optimization_barrier(jnp.sum(resid * resid, axis=-1, keepdims=True))
            direction = resid + norm_next / norm_now * direction
            norm_now = norm_next
        scores = jnp.dot(solution, key_c.T, precision=HIGH) * weights
        readout = lead * jnp.dot(solution, state_vk.T, precision=HIGH) + jnp.dot(scores, value_c, precision=HIGH)
        total = within[-1]
        factor = jnp.exp(total - within) * beta_c
        new_kk = jnp.exp(total) * state_kk + jnp.dot((key_c * factor[:, None]).T, key_c, precision=HIGH)
        new_vk = jnp.exp(total) * state_vk + jnp.dot((value_c * factor[:, None]).T, key_c, precision=HIGH)
        return ((new_kk, new_vk), readout)
    start = (jnp.zeros((HD, HD), jnp.float32), jnp.zeros((HD, HD), jnp.float32))
    final, outputs = lax.scan(one_block, start, (query_blocks, key_blocks, value_blocks, decay_blocks, beta_blocks))
    return outputs.reshape(TOKENS, HD)

def reference(features, gate_weight, queries, keys, values, log_decay, ridge):
    logits = jnp.dot(features, gate_weight, preferred_element_type=jnp.float32)
    beta = jax.nn.sigmoid(logits)

    def separate_heads(arr):
        return arr.astype(jnp.float32).reshape(TOKENS, H, HD).transpose(1, 0, 2)
    outputs = lax.map(head_pass, (separate_heads(queries), separate_heads(keys), separate_heads(values), log_decay.T, beta.T, ridge))
    return outputs.transpose(1, 0, 2).reshape(TOKENS, H * HD).astype(jnp.bfloat16)
```

```python
import functools

import jax
import jax.numpy as jnp
from jax import lax
from jax.experimental import pallas as pl
from jax.experimental.pallas import tpu as pltpu
from jax.sharding import PartitionSpec as P

CG_STEPS = 4
BLOCK = 256
MESH = pl.DeviceIdType.MESH
F32 = jnp.float32
BF16 = jnp.bfloat16


def nn(a, b):
    return jnp.dot(a, b, preferred_element_type=F32)


def nt(a, b):
    return lax.dot_general(a, b, (((1,), (1,)), ((), ())), preferred_element_type=F32)


def tn(a, b):
    return lax.dot_general(a, b, (((0,), (0,)), ((), ())), preferred_element_type=F32)


def split(a):
    hi = a.astype(BF16)
    return hi, (a - hi.astype(F32)).astype(BF16)


def column_sums(sq):
    ones = jnp.ones((8, sq.shape[1]), BF16)
    hi, lo = split(sq)
    return nt(ones, hi) + nt(ones, lo)


def kernel(
    ny, nz, nh, feat, gw, q_ref, k_ref, v_ref, ld_ref, ridge_ref, out_ref,
    gsend, grecv, sbuf, rbuf, ybuf, yrecv, tbuf, trecv, w1_ref, w2_ref, s1_ref, in1_ref,
    gs_sem, gr_sem, ss_sem, sr_sem, ys_sem, yr_sem, ts_sem, tr_sem,
):
    rows = q_ref.shape[0]
    heads = ridge_ref.shape[0]
    width = ridge_ref.shape[1]
    blocks = rows // BLOCK
    part = width // nz
    seq = lax.axis_index("seq")
    me_h = lax.axis_index("head")
    me_y = seq // nz
    me_z = seq % nz

    barrier = pltpu.get_barrier_semaphore()
    for d in range(1, nh):
        pl.semaphore_signal(barrier, inc=1, device_id={"head": (me_h + d) % nh}, device_id_type=MESH)
    order = sorted(range(1, nz), key=lambda d: -min(d, nz - d))
    for d in order:
        pl.semaphore_signal(
            barrier, inc=1, device_id={"seq": me_y * nz + (me_z + d) % nz}, device_id_type=MESH
        )
    for d in range(1, ny):
        pl.semaphore_signal(
            barrier, inc=1, device_id={"seq": ((me_y + d) % ny) * nz + me_z}, device_id_type=MESH
        )

    partial = nt(gw[...], feat[...])
    for j in range(nh):
        gsend[j] = partial[heads * j : heads * (j + 1)]

    pl.semaphore_wait(barrier, nh - 1 + nz - 1 + ny - 1)

    gate_copies = []
    for d in range(1, nh):
        to = (me_h + d) % nh
        c = pltpu.make_async_remote_copy(
            src_ref=gsend.at[to], dst_ref=grecv.at[me_h], send_sem=gs_sem.at[d],
            recv_sem=gr_sem.at[d], device_id={"head": to}, device_id_type=MESH,
        )
        c.start()
        gate_copies.append(c)
    grecv[me_h] = gsend[me_h]

    within = jnp.concatenate([ld_ref[...]] * (8 // heads), axis=0)
    place = lax.broadcasted_iota(jnp.int32, (8, rows), 1) % BLOCK
    step = 1
    while step < BLOCK:
        within = within + jnp.where(place >= step, pltpu.roll(within, step, 1), 0.0)
        step *= 2
    ksq = []
    for h in range(heads):
        kf = k_ref[:, h * width : (h + 1) * width].astype(F32)
        ksq.append(column_sums(kf * kf)[0:1])
    knorm = jnp.sqrt(jnp.concatenate(ksq, axis=0) + 1e-06)
    kinv = 1.0 / knorm
    within = within[0:heads]
    ends = [within[:, (b + 1) * BLOCK - 1 : (b + 1) * BLOCK] for b in range(blocks)]
    total_row = jnp.concatenate([jnp.broadcast_to(e, (heads, BLOCK)) for e in ends], axis=1)
    tail = jnp.exp(total_row - within)
    ltot = functools.reduce(lambda a, b: a + b, ends)

    qunit, qinv = [], []
    for h in range(heads):
        qf = q_ref[:, h * width : (h + 1) * width].astype(F32)
        root = jnp.sqrt(jnp.sum(qf * qf, axis=-1, keepdims=True) + 1e-06)
        qunit.append(qf / root)
        qinv.append(1.0 / root)

    for c in gate_copies:
        c.wait()
    logits = grecv[0]
    for j in range(1, nh):
        logits = logits + grecv[j]
    beta = 1.0 / (1.0 + jnp.exp(-logits))
    vfac = tail * beta * kinv
    kfac = vfac * kinv
    rows8 = jnp.concatenate([kfac, vfac, within, jnp.exp(within)], axis=0)
    cols = jnp.transpose(jnp.concatenate([rows8] * (128 // rows8.shape[0]), axis=0))

    def col(kind, h, b):
        return cols[b * BLOCK : (b + 1) * BLOCK, kind * heads + h : kind * heads + h + 1]

    def keys(h, b):
        return k_ref[b * BLOCK : (b + 1) * BLOCK, h * width : (h + 1) * width]

    def values(h, b):
        return v_ref[b * BLOCK : (b + 1) * BLOCK, h * width : (h + 1) * width]

    updates = []
    for h in range(heads):
        ups = []
        for b in range(blocks):
            kb = keys(h, b)
            fk = kb.astype(F32) * col(0, h, b)
            fv = values(h, b).astype(F32) * col(1, h, b)
            hi, lo = split(jnp.concatenate([fk, fv], axis=1))
            ups.append(tn(kb, hi) + tn(kb, lo))
        updates.append(ups)
        total = ups[0]
        for b in range(1, blocks):
            total = total * jnp.exp(ends[b][h : h + 1]) + ups[b]
        for c in range(nz):
            sbuf[h, c, 0:part] = total[c * part : (c + 1) * part, 0:width]
            sbuf[h, c, part : 2 * part] = total[c * part : (c + 1) * part, width:]
            sbuf[h, c, 2 * part : 2 * part + 1] = jnp.broadcast_to(ltot[h : h + 1], (1, width))

    msg = 2 * part + 1
    sends = []
    for h in range(heads):
        for d in order:
            to = (me_z + d) % nz
            c = pltpu.make_async_remote_copy(
                src_ref=sbuf.at[h, to, pl.ds(0, msg)], dst_ref=rbuf.at[h, me_z, pl.ds(0, msg)],
                send_sem=ss_sem.at[h, d], recv_sem=sr_sem.at[h, d],
                device_id={"seq": me_y * nz + to}, device_id_type=MESH,
            )
            c.start()
            sends.append(c)
        rbuf[h, me_z] = sbuf[h, me_z]

    lower = lax.broadcasted_iota(jnp.int32, (BLOCK, BLOCK), 0) >= lax.broadcasted_iota(
        jnp.int32, (BLOCK, BLOCK), 1
    )
    row1 = beta * kinv * kinv
    row2 = beta * kinv
    for h in range(heads):
        for b in range(blocks):
            i = h * blocks + b
            sl = slice(b * BLOCK, (b + 1) * BLOCK)
            spread = col(2, h, b) - within[h : h + 1, sl]
            decay = jnp.where(lower, jnp.exp(jnp.minimum(spread, 0.0)), 0.0)
            w1 = decay * row1[h : h + 1, sl]
            w1_ref[i] = w1
            w2_ref[i] = decay * row2[h : h + 1, sl]
            kb = keys(h, b)
            s = nt(q_ref[sl, h * width : (h + 1) * width], kb) * qinv[h][sl]
            s1_ref[i] = s
            hi, lo = split(s * w1)
            in1_ref[i] = nn(hi, kb) + nn(lo, kb)

    y_copies = []
    for h in range(heads):
        for d in range(1, nz):
            sends[h * (nz - 1) + d - 1].wait()
        state = jnp.zeros((2 * part, width), F32)
        reach = jnp.zeros((1, width), F32)
        for z in range(nz):
            tbuf[h, z, 0 : 2 * part] = state
            tbuf[h, z, 2 * part : 2 * part + 1] = reach
            log = rbuf[h, z, 2 * part : 2 * part + 1]
            state = jnp.exp(log) * state + rbuf[h, z, 0 : 2 * part]
            reach = reach + log
        ybuf[h, 0 : 2 * part] = state
        ybuf[h, 2 * part : 2 * part + 1] = reach
        yrecv[h, me_y] = ybuf[h]
        for d in range(1, ny):
            to = (me_y + d) % ny
            c = pltpu.make_async_remote_copy(
                src_ref=ybuf.at[h, pl.ds(0, msg)], dst_ref=yrecv.at[h, me_y, pl.ds(0, msg)],
                send_sem=ys_sem.at[h, d], recv_sem=yr_sem.at[h, d],
                device_id={"seq": to * nz + me_z}, device_id_type=MESH,
            )
            c.start()
            y_copies.append(c)

    returns = []
    for h in range(heads):
        for d in range(1, ny):
            y_copies[h * (ny - 1) + d - 1].wait()
        carry = jnp.zeros((2 * part, width), F32)
        for y in range(ny):
            new = jnp.exp(yrecv[h, y, 2 * part : 2 * part + 1]) * carry + yrecv[h, y, 0 : 2 * part]
            carry = jnp.where(y < me_y, new, carry)
        for z in range(nz):
            tbuf[h, z, 0 : 2 * part] = (
                tbuf[h, z, 0 : 2 * part] + jnp.exp(tbuf[h, z, 2 * part : 2 * part + 1]) * carry
            )
        for d in order:
            to = (me_z + d) % nz
            c = pltpu.make_async_remote_copy(
                src_ref=tbuf.at[h, to, pl.ds(0, 2 * part)],
                dst_ref=trecv.at[h, me_z, pl.ds(0, 2 * part)],
                send_sem=ts_sem.at[h, d], recv_sem=tr_sem.at[h, d],
                device_id={"seq": me_y * nz + to}, device_id_type=MESH,
            )
            c.start()
            returns.append(c)
        trecv[h, me_z] = tbuf[h, me_z, 0 : 2 * part]

    for h in range(heads):
        for d in range(1, nz):
            returns[h * (nz - 1) + d - 1].wait()
        start = jnp.concatenate(
            [
                trecv[h, :, 0:part].reshape(width, width),
                trecv[h, :, part : 2 * part].reshape(width, width),
            ],
            axis=1,
        )
        ridge = ridge_ref[h : h + 1]
        for b in range(blocks):
            i = h * blocks + b
            sl = slice(b * BLOCK, (b + 1) * BLOCK)
            if b > 0:
                start = start * jnp.exp(ends[b - 1][h : h + 1]) + updates[h][b - 1]
            hi, lo = split(start)
            khi, klo, vhi, vlo = hi[:, :width], lo[:, :width], hi[:, width:], lo[:, width:]
            zero = jnp.zeros_like(klo)
            kk_pair = jnp.concatenate(
                [jnp.concatenate([khi, klo], axis=1), jnp.concatenate([khi, zero], axis=1)], axis=0
            )
            vk_pair = jnp.concatenate(
                [jnp.concatenate([vhi, vlo], axis=1), jnp.concatenate([vhi, zero], axis=1)], axis=0
            )
            kb = keys(h, b)
            vb = values(h, b)
            k_wide = jnp.concatenate([kb, kb], axis=1)
            k_tall = jnp.concatenate([kb, kb], axis=0)
            v_tall = jnp.concatenate([vb, vb], axis=0)
            lead = col(3, h, b)
            w1 = w1_ref[i]
            p = qunit[h][sl]
            r = p
            norm = jnp.sum(r * r, axis=-1, keepdims=True)
            s = s1_ref[i]
            both = nn(q_ref[sl, h * width : (h + 1) * width], kk_pair[:width])
            state_part = (both[:, :width] + both[:, width:]) * (lead * qinv[h][sl])
            x = jnp.zeros_like(p)
            s_sum = jnp.zeros_like(s)
            for step in range(CG_STEPS):
                if step > 0:
                    ph, plo = split(p)
                    pair = jnp.concatenate([ph, plo], axis=1)
                    both = nn(pair, kk_pair)
                    state_part = lead * (both[:, :width] + both[:, width:])
                    s = nt(pair, k_wide)
                near = state_part + ridge * p
                sw = s * w1
                if step == CG_STEPS - 1:
                    energy = jnp.sum(p * near, axis=-1, keepdims=True) + jnp.sum(
                        s * sw, axis=-1, keepdims=True
                    )
                    alpha = norm / energy
                    x = x + alpha * p
                    s_sum = s_sum + alpha * s
                    break
                if step == 0:
                    image = near + in1_ref[i]
                else:
                    sh, slo = split(sw)
                    image = near + nn(jnp.concatenate([sh, slo], axis=1), k_tall)
                alpha = norm / jnp.sum(p * image, axis=-1, keepdims=True)
                x = x + alpha * p
                s_sum = s_sum + alpha * s
                r = r - alpha * image
                after = jnp.sum(r * r, axis=-1, keepdims=True)
                p = r + (after / norm) * p
                norm = after
            xh, xlo = split(x)
            both = nn(jnp.concatenate([xh, xlo], axis=1), vk_pair)
            sh, slo = split(s_sum * w2_ref[i])
            mixed = lead * (both[:, :width] + both[:, width:]) + nn(
                jnp.concatenate([sh, slo], axis=1), v_tall
            )
            out_ref[sl, h * width : (h + 1) * width] = mixed.astype(BF16)


def body(ny, nz, nh, features, gate_weight, queries, keys, values, log_decay, ridge):
    rows = queries.shape[0]
    heads, width = ridge.shape
    blocks = rows // BLOCK
    part = width // nz
    vmem = pl.BlockSpec(memory_space=pltpu.VMEM)
    pad = -(-(2 * part + 1) // 8) * 8
    dma = pltpu.SemaphoreType.DMA
    return pl.pallas_call(
        functools.partial(kernel, ny, nz, nh),
        out_shape=jax.ShapeDtypeStruct((rows, heads * width), BF16),
        in_specs=[vmem] * 7,
        out_specs=vmem,
        scratch_shapes=[
            pltpu.VMEM((nh, heads, rows), F32),
            pltpu.VMEM((nh, heads, rows), F32),
            pltpu.VMEM((heads, nz, pad, width), F32),
            pltpu.VMEM((heads, nz, pad, width), F32),
            pltpu.VMEM((heads, pad, width), F32),
            pltpu.VMEM((heads, ny, pad, width), F32),
            pltpu.VMEM((heads, nz, pad, width), F32),
            pltpu.VMEM((heads, nz, 2 * part, width), F32),
            pltpu.VMEM((heads * blocks, BLOCK, BLOCK), F32),
            pltpu.VMEM((heads * blocks, BLOCK, BLOCK), F32),
            pltpu.VMEM((heads * blocks, BLOCK, BLOCK), F32),
            pltpu.VMEM((heads * blocks, BLOCK, width), F32),
            dma((nh,)), dma((nh,)), dma((heads, nz)), dma((heads, nz)),
            dma((heads, ny)), dma((heads, ny)), dma((heads, nz)), dma((heads, nz)),
        ],
        compiler_params=pltpu.CompilerParams(collective_id=0, has_side_effects=True),
        name="mesa",
    )(features, gate_weight.T, queries, keys, values, log_decay.T, ridge)


def solution(mesh):
    seq, nh = mesh.shape["seq"], mesh.shape["head"]
    nz = 16 if seq >= 64 else seq // 2
    placed = (
        P("seq", "head"),
        P("head", None),
        P("seq", "head"),
        P("seq", "head"),
        P("seq", "head"),
        P("seq", "head"),
        P("head", None),
    )
    return jax.shard_map(
        functools.partial(body, seq // nz, nz, nh),
        mesh=mesh, in_specs=placed, out_specs=P("seq", "head"), check_vma=False,
    )
```

```python
import functools

import jax
import jax.numpy as jnp
from jax import lax
from jax.experimental import pallas as pl
from jax.experimental.pallas import tpu as pltpu
from jax.sharding import PartitionSpec as P

CG_STEPS = 4
BLOCK = 256
MESH = pl.DeviceIdType.MESH
F32 = jnp.float32
BF16 = jnp.bfloat16


def nn(a, b):
    return jnp.dot(a, b, preferred_element_type=F32)


def nt(a, b):
    return lax.dot_general(a, b, (((1,), (1,)), ((), ())), preferred_element_type=F32)


def tn(a, b):
    return lax.dot_general(a, b, (((0,), (0,)), ((), ())), preferred_element_type=F32)


def split(a):
    hi = a.astype(BF16)
    return hi, (a - hi.astype(F32)).astype(BF16)


def column_sums(sq):
    ones = jnp.ones((8, sq.shape[1]), BF16)
    hi, lo = split(sq)
    return nt(ones, hi) + nt(ones, lo)


def pack(total, width):
    half = width // 2
    lane = lax.broadcasted_iota(jnp.int32, (half, width), 1)
    row = lax.broadcasted_iota(jnp.int32, (half, width), 0)
    top = total[0:half, 0:width]
    turned = pltpu.roll(total[half:width, 0:width], half, 1)
    folded = jnp.where(lane >= row, top, turned)
    diagonal = jnp.sum(jnp.where(lane == row, turned, 0.0), axis=0, keepdims=True)
    return total[:, width:], folded, diagonal


def unpack(vkt, folded, diagonal, width):
    half = width // 2
    lane = lax.broadcasted_iota(jnp.int32, (half, width), 1)
    row = lax.broadcasted_iota(jnp.int32, (half, width), 0)
    flipped = jnp.transpose(jnp.concatenate([folded, jnp.zeros_like(folded)], axis=0))
    top = jnp.where(lane >= row, folded, flipped[0:half])
    corner = jnp.where(lane == row, diagonal, jnp.where(lane < row, folded, flipped[0:half]))
    bottom = jnp.where(lane < half, flipped[half:width], pltpu.roll(corner, half, 1))
    return jnp.concatenate([jnp.concatenate([top, bottom], axis=0), vkt], axis=1)


def kernel(
    ny, nz, nh, feat_hbm, gw_hbm, q_hbm, k_hbm, v_hbm, ld_hbm, ridge_hbm, out_ref,
    feat, gw, q_ref, k_ref, v_ref, ld_ref, ridge_ref,
    gsend, grecv, sbuf, rbuf, ybuf, yrecv, tbuf, trecv, w1_ref, w2_ref, s1_ref, in1_ref,
    in_sem, ready, gs_sem, gr_sem, ss_sem, sr_sem, ys_sem, yr_sem, ts_sem, tr_sem,
):
    rows = q_ref.shape[0]
    heads = ridge_ref.shape[0]
    width = ridge_ref.shape[1]
    blocks = rows // BLOCK
    part = width // nz
    fold = part // 2
    body_rows = part + fold + 1
    seq = lax.axis_index("seq")
    me_h = lax.axis_index("head")
    me_y = seq // nz
    me_z = seq % nz

    def at_z(d):
        return {"seq": me_y * nz + (me_z + d + nz) % nz}

    def at_y(d):
        return {"seq": ((me_y + d) % ny) * nz + me_z}

    def signal(sem, where):
        pl.semaphore_signal(sem, inc=1, device_id=where, device_id_type=MESH)

    def send(src, dst, sem_out, sem_in, where):
        c = pltpu.make_async_remote_copy(
            src_ref=src, dst_ref=dst, send_sem=sem_out, recv_sem=sem_in,
            device_id=where, device_id_type=MESH,
        )
        c.start()
        return c

    barrier = pltpu.get_barrier_semaphore()
    for d in range(1, nh):
        signal(barrier, {"head": (me_h + d) % nh})
    for d in (1, -1):
        signal(barrier, at_z(d))
    for d in range(1, ny):
        signal(barrier, at_y(d))

    loads = []
    for i, (src, dst) in enumerate(
        [
            (gw_hbm, gw), (feat_hbm, feat), (ld_hbm, ld_ref), (k_hbm, k_ref),
            (q_hbm, q_ref), (v_hbm, v_ref), (ridge_hbm, ridge_ref),
        ]
    ):
        c = pltpu.make_async_copy(src, dst, in_sem.at[i])
        c.start()
        loads.append(c)
    loads[0].wait()
    loads[1].wait()
    partial = nt(gw[...], feat[...])
    for j in range(nh):
        gsend[j] = partial[heads * j : heads * (j + 1)]

    pl.semaphore_wait(barrier, nh - 1 + 2 + ny - 1)

    signal(ready.at[0], at_z(1))
    signal(ready.at[0], at_z(-1))
    gate_copies = []
    for d in range(1, nh):
        to = (me_h + d) % nh
        gate_copies.append(
            send(gsend.at[to], grecv.at[me_h], gs_sem.at[d], gr_sem.at[d], {"head": to})
        )
    grecv[me_h] = gsend[me_h]

    loads[2].wait()
    within = jnp.concatenate([ld_ref[...]] * (8 // heads), axis=0)
    place = lax.broadcasted_iota(jnp.int32, (8, rows), 1) % BLOCK
    step = 1
    while step < BLOCK:
        within = within + jnp.where(place >= step, pltpu.roll(within, step, 1), 0.0)
        step *= 2
    loads[3].wait()
    ksq = []
    for h in range(heads):
        kf = k_ref[:, h * width : (h + 1) * width].astype(F32)
        ksq.append(column_sums(kf * kf)[0:1])
    knorm = jnp.sqrt(jnp.concatenate(ksq, axis=0) + 1e-06)
    kinv = 1.0 / knorm
    within = within[0:heads]
    ends = [within[:, (b + 1) * BLOCK - 1 : (b + 1) * BLOCK] for b in range(blocks)]
    total_row = jnp.concatenate([jnp.broadcast_to(e, (heads, BLOCK)) for e in ends], axis=1)
    tail = jnp.exp(total_row - within)
    ltot = functools.reduce(lambda a, b: a + b, ends)

    reach = 1
    turn = 0
    while 2 * reach <= nz // 2:
        pl.semaphore_wait(ready.at[turn], 2)
        reach *= 2
        turn += 1
        if 2 * reach <= nz // 2:
            signal(ready.at[turn], at_z(reach))
            signal(ready.at[turn], at_z(-reach))

    loads[5].wait()
    for c in gate_copies:
        c.wait()
    logits = grecv[0]
    for j in range(1, nh):
        logits = logits + grecv[j]
    beta = 1.0 / (1.0 + jnp.exp(-logits))
    vfac = tail * beta * kinv
    kfac = vfac * kinv
    rows8 = jnp.concatenate([kfac, vfac, within, jnp.exp(within)], axis=0)
    cols = jnp.transpose(jnp.concatenate([rows8] * (128 // rows8.shape[0]), axis=0))

    def col(kind, h, b):
        return cols[b * BLOCK : (b + 1) * BLOCK, kind * heads + h : kind * heads + h + 1]

    def keys(h, b):
        return k_ref[b * BLOCK : (b + 1) * BLOCK, h * width : (h + 1) * width]

    def values(h, b):
        return v_ref[b * BLOCK : (b + 1) * BLOCK, h * width : (h + 1) * width]

    order = sorted(range(1, nz), key=lambda d: -min(d, nz - d))
    lane_row = lax.broadcasted_iota(jnp.int32, (1, width), 1)
    updates, sends = [], []
    for h in range(heads):
        ups = []
        for b in range(blocks):
            kb = keys(h, b)
            fk = kb.astype(F32) * col(0, h, b)
            fv = values(h, b).astype(F32) * col(1, h, b)
            hi, lo = split(jnp.concatenate([fk, fv], axis=1))
            ups.append(tn(kb, hi) + tn(kb, lo))
        updates.append(ups)
        total = ups[0]
        for b in range(1, blocks):
            total = total * jnp.exp(ends[b][h : h + 1]) + ups[b]
        vkt, folded, diagonal = pack(total, width)
        last = jnp.where(lane_row < width // 2, diagonal, ltot[h : h + 1])
        for c in range(nz):
            sbuf[h, c, 0:part] = vkt[c * part : (c + 1) * part]
            sbuf[h, c, part : part + fold] = folded[c * fold : (c + 1) * fold]
            sbuf[h, c, part + fold : body_rows] = last
        out = []
        for d in order:
            to = (me_z + d) % nz
            out.append(
                send(
                    sbuf.at[h, to, pl.ds(0, body_rows)], rbuf.at[h, me_z, pl.ds(0, body_rows)],
                    ss_sem.at[h, d], sr_sem.at[h, d], at_z(d),
                )
            )
        sends.append(out)
        rbuf[h, me_z] = sbuf[h, me_z]

    lower = lax.broadcasted_iota(jnp.int32, (BLOCK, BLOCK), 0) >= lax.broadcasted_iota(
        jnp.int32, (BLOCK, BLOCK), 1
    )
    loads[4].wait()
    loads[6].wait()
    qunit, qinv = [], []
    for h in range(heads):
        qf = q_ref[:, h * width : (h + 1) * width].astype(F32)
        root = jnp.sqrt(jnp.sum(qf * qf, axis=-1, keepdims=True) + 1e-06)
        qunit.append(qf / root)
        qinv.append(1.0 / root)
    row1 = beta * kinv * kinv
    row2 = beta * kinv

    def prepare(h):
        for b in range(blocks):
            i = h * blocks + b
            sl = slice(b * BLOCK, (b + 1) * BLOCK)
            spread = col(2, h, b) - within[h : h + 1, sl]
            decay = jnp.where(lower, jnp.exp(jnp.minimum(spread, 0.0)), 0.0)
            w1 = decay * row1[h : h + 1, sl]
            w1_ref[i] = w1
            w2_ref[i] = decay * row2[h : h + 1, sl]
            kb = keys(h, b)
            s = nt(q_ref[sl, h * width : (h + 1) * width], kb) * qinv[h][sl]
            s1_ref[i] = s
            hi, lo = split(s * w1)
            in1_ref[i] = nn(hi, kb) + nn(lo, kb)

    def row_prefix(h):
        for c in sends[h]:
            c.wait()
        state = jnp.zeros((body_rows, width), F32)
        gone = jnp.zeros((1, 1), F32)
        logs = []
        for z in range(nz):
            tbuf[h, z, 0:body_rows] = state
            logs.append(gone)
            chunk = rbuf[h, z, 0:body_rows]
            log = chunk[part + fold : body_rows, width - 1 : width]
            state = jnp.exp(log) * state + chunk
            gone = gone + log
        ybuf[h, 0:body_rows] = jnp.where(
            (lax.broadcasted_iota(jnp.int32, (body_rows, width), 0) == body_rows - 1)
            & (lax.broadcasted_iota(jnp.int32, (body_rows, width), 1) >= width // 2),
            gone, state,
        )
        yrecv[h, me_y] = ybuf[h]
        copies = [
            send(
                ybuf.at[h, pl.ds(0, body_rows)], yrecv.at[h, me_y, pl.ds(0, body_rows)],
                ys_sem.at[h, d], yr_sem.at[h, d], at_y(d),
            )
            for d in range(1, ny)
        ]
        return logs, copies

    def give_back(h, logs, copies):
        for c in copies:
            c.wait()
        carry = jnp.zeros((body_rows, width), F32)
        for y in range(ny):
            chunk = yrecv[h, y, 0:body_rows]
            new = jnp.exp(chunk[part + fold : body_rows, width - 1 : width]) * carry + chunk
            carry = jnp.where(y < me_y, new, carry)
        for z in range(nz):
            tbuf[h, z, 0:body_rows] = tbuf[h, z, 0:body_rows] + jnp.exp(logs[z]) * carry
        out = []
        for d in order:
            to = (me_z + d) % nz
            out.append(
                send(
                    tbuf.at[h, to, pl.ds(0, body_rows)], trecv.at[h, me_z, pl.ds(0, body_rows)],
                    ts_sem.at[h, d], tr_sem.at[h, d], at_z(d),
                )
            )
        trecv[h, me_z] = tbuf[h, me_z]
        return out

    def solve(h, returns):
        for c in returns:
            c.wait()
        start = unpack(
            trecv[h, :, 0:part].reshape(width, width),
            jnp.concatenate([trecv[h, c, part : part + fold] for c in range(nz)], axis=0),
            trecv[h, 0, part + fold : body_rows],
            width,
        )
        ridge = ridge_ref[h : h + 1]
        for b in range(blocks):
            i = h * blocks + b
            sl = slice(b * BLOCK, (b + 1) * BLOCK)
            if b > 0:
                start = start * jnp.exp(ends[b - 1][h : h + 1]) + updates[h][b - 1]
            hi, lo = split(start)
            khi, klo, vhi, vlo = hi[:, :width], lo[:, :width], hi[:, width:], lo[:, width:]
            zero = jnp.zeros_like(klo)
            kk_pair = jnp.concatenate(
                [jnp.concatenate([khi, klo], axis=1), jnp.concatenate([khi, zero], axis=1)], axis=0
            )
            vk_pair = jnp.concatenate(
                [jnp.concatenate([vhi, vlo], axis=1), jnp.concatenate([vhi, zero], axis=1)], axis=0
            )
            kb = keys(h, b)
            vb = values(h, b)
            k_wide = jnp.concatenate([kb, kb], axis=1)
            k_tall = jnp.concatenate([kb, kb], axis=0)
            v_tall = jnp.concatenate([vb, vb], axis=0)
            lead = col(3, h, b)
            w1 = w1_ref[i]
            p = qunit[h][sl]
            r = p
            norm = jnp.sum(r * r, axis=-1, keepdims=True)
            s = s1_ref[i]
            both = nn(q_ref[sl, h * width : (h + 1) * width], kk_pair[:width])
            state_part = (both[:, :width] + both[:, width:]) * (lead * qinv[h][sl])
            x = jnp.zeros_like(p)
            s_sum = jnp.zeros_like(s)
            for step in range(CG_STEPS):
                if step > 0:
                    ph, plo = split(p)
                    pair = jnp.concatenate([ph, plo], axis=1)
                    both = nn(pair, kk_pair)
                    state_part = lead * (both[:, :width] + both[:, width:])
                    s = nt(pair, k_wide)
                near = state_part + ridge * p
                sw = s * w1
                if step == CG_STEPS - 1:
                    energy = jnp.sum(p * near, axis=-1, keepdims=True) + jnp.sum(
                        s * sw, axis=-1, keepdims=True
                    )
                    alpha = norm / energy
                    x = x + alpha * p
                    s_sum = s_sum + alpha * s
                    break
                if step == 0:
                    image = near + in1_ref[i]
                else:
                    sh, slo = split(sw)
                    image = near + nn(jnp.concatenate([sh, slo], axis=1), k_tall)
                alpha = norm / jnp.sum(p * image, axis=-1, keepdims=True)
                x = x + alpha * p
                s_sum = s_sum + alpha * s
                r = r - alpha * image
                after = jnp.sum(r * r, axis=-1, keepdims=True)
                p = r + (after / norm) * p
                norm = after
            xh, xlo = split(x)
            both = nn(jnp.concatenate([xh, xlo], axis=1), vk_pair)
            sh, slo = split(s_sum * w2_ref[i])
            mixed = lead * (both[:, :width] + both[:, width:]) + nn(
                jnp.concatenate([sh, slo], axis=1), v_tall
            )
            out_ref[sl, h * width : (h + 1) * width] = mixed.astype(BF16)

    prepare(0)
    logs0, copies0 = row_prefix(0)
    pending = [give_back(0, logs0, copies0)]
    for h in range(1, heads):
        prepare(h)
        logs, copies = row_prefix(h)
        pending.append(give_back(h, logs, copies))
    for h in range(heads):
        solve(h, pending[h])


def body(ny, nz, nh, features, gate_weight, queries, keys, values, log_decay, ridge):
    rows, columns = queries.shape
    heads, width = ridge.shape
    blocks = rows // BLOCK
    part = width // nz
    vmem = pl.BlockSpec(memory_space=pltpu.VMEM)
    pad = -(-(part + part // 2 + 1) // 8) * 8
    dma = pltpu.SemaphoreType.DMA
    ops = (features, gate_weight.T, queries, keys, values, log_decay.T, ridge)
    return pl.pallas_call(
        functools.partial(kernel, ny, nz, nh),
        out_shape=jax.ShapeDtypeStruct((rows, columns), BF16),
        in_specs=[pl.BlockSpec(memory_space=pl.ANY)] * 7,
        out_specs=vmem,
        scratch_shapes=[pltpu.VMEM(o.shape, o.dtype) for o in ops]
        + [
            pltpu.VMEM((nh, heads, rows), F32),
            pltpu.VMEM((nh, heads, rows), F32),
            pltpu.VMEM((heads, nz, pad, width), F32),
            pltpu.VMEM((heads, nz, pad, width), F32),
            pltpu.VMEM((heads, pad, width), F32),
            pltpu.VMEM((heads, ny, pad, width), F32),
            pltpu.VMEM((heads, nz, pad, width), F32),
            pltpu.VMEM((heads, nz, pad, width), F32),
            pltpu.VMEM((heads * blocks, BLOCK, BLOCK), F32),
            pltpu.VMEM((heads * blocks, BLOCK, BLOCK), F32),
            pltpu.VMEM((heads * blocks, BLOCK, BLOCK), F32),
            pltpu.VMEM((heads * blocks, BLOCK, width), F32),
            dma((7,)), pltpu.SemaphoreType.REGULAR((4,)),
            dma((nh,)), dma((nh,)), dma((heads, nz)), dma((heads, nz)),
            dma((heads, ny)), dma((heads, ny)), dma((heads, nz)), dma((heads, nz)),
        ],
        compiler_params=pltpu.CompilerParams(collective_id=0, has_side_effects=True),
        name="mesa",
    )(*ops)


def solution(mesh):
    seq, nh = mesh.shape["seq"], mesh.shape["head"]
    nz = 16 if seq >= 64 else seq // 2
    placed = (
        P("seq", "head"),
        P("head", None),
        P("seq", "head"),
        P("seq", "head"),
        P("seq", "head"),
        P("seq", "head"),
        P("head", None),
    )
    return jax.shard_map(
        functools.partial(body, seq // nz, nz, nh),
        mesh=mesh, in_specs=placed, out_specs=P("seq", "head"), check_vma=False,
    )
```

```python
import functools

import jax
import jax.numpy as jnp
from jax import lax
from jax.experimental import pallas as pl
from jax.experimental.pallas import tpu as pltpu
from jax.sharding import PartitionSpec as P

CG_STEPS = 4
BLOCK = 256
MESH = pl.DeviceIdType.MESH
F32 = jnp.float32
BF16 = jnp.bfloat16


def nn(a, b):
    return jnp.dot(a, b, preferred_element_type=F32)


def nt(a, b):
    return lax.dot_general(a, b, (((1,), (1,)), ((), ())), preferred_element_type=F32)


def tn(a, b):
    return lax.dot_general(a, b, (((0,), (0,)), ((), ())), preferred_element_type=F32)


def split(a):
    hi = a.astype(BF16)
    return hi, (a - hi.astype(F32)).astype(BF16)


def column_sums(sq):
    ones = jnp.ones((8, sq.shape[1]), BF16)
    hi, lo = split(sq)
    return nt(ones, hi) + nt(ones, lo)


def pack(total, width):
    half = width // 2
    lane = lax.broadcasted_iota(jnp.int32, (half, width), 1)
    row = lax.broadcasted_iota(jnp.int32, (half, width), 0)
    top = total[0:half]
    turned = pltpu.roll(total[half:width], half, 1)
    folded = jnp.where(lane >= row, top, turned)
    diagonal = jnp.sum(jnp.where(lane == row, turned, 0.0), axis=0, keepdims=True)
    return folded, diagonal


def unpack(folded, diagonal, width):
    half = width // 2
    lane = lax.broadcasted_iota(jnp.int32, (half, width), 1)
    row = lax.broadcasted_iota(jnp.int32, (half, width), 0)
    flipped = jnp.transpose(jnp.concatenate([folded, jnp.zeros_like(folded)], axis=0))
    top = jnp.where(lane >= row, folded, flipped[0:half])
    corner = jnp.where(lane == row, diagonal, jnp.where(lane < row, folded, flipped[0:half]))
    bottom = jnp.where(lane < half, flipped[half:width], pltpu.roll(corner, half, 1))
    return jnp.concatenate([top, bottom], axis=0)


def kernel(
    ny, nz, nh, feat_hbm, gw_hbm, q_hbm, k_hbm, v_hbm, ld_hbm, ridge_hbm, out_ref,
    feat, gw, q_ref, k_ref, v_ref, ld_ref, ridge_ref,
    gsend, grecv, sbuf, rbuf, ybuf, yrecv, carry_ref, tbuf, trecv, kt_ref, w1_ref, w2_ref, s1_ref, in1_ref,
    in_sem, ready, gs_sem, gr_sem, ss_sem, sr_sem, ys_sem, yr_sem, ts_sem, tr_sem,
):
    rows = q_ref.shape[0]
    heads = ridge_ref.shape[0]
    width = ridge_ref.shape[1]
    blocks = rows // BLOCK
    part = width // nz
    fold = part // 2
    counts = (heads * (fold + 1), heads * part)
    seq = lax.axis_index("seq")
    me_h = lax.axis_index("head")
    me_y = seq // nz
    me_z = seq % nz

    def at_z(d):
        return {"seq": me_y * nz + (me_z + d + nz) % nz}

    def at_y(d):
        return {"seq": ((me_y + d) % ny) * nz + me_z}

    def signal(sem, where):
        pl.semaphore_signal(sem, inc=1, device_id=where, device_id_type=MESH)

    def send(src, dst, sem_out, sem_in, where):
        c = pltpu.make_async_remote_copy(
            src_ref=src, dst_ref=dst, send_sem=sem_out, recv_sem=sem_in,
            device_id=where, device_id_type=MESH,
        )
        c.start()
        return c

    barrier = pltpu.get_barrier_semaphore()
    for d in range(1, nh):
        signal(barrier, {"head": (me_h + d) % nh})
    near = sorted({d % nz for d in (1, -1, 2, -2)} - {0})
    for d in near:
        signal(barrier, at_z(d))
    for d in range(1, ny):
        signal(barrier, at_y(d))

    loads = []
    for i, (src, dst) in enumerate(
        [
            (gw_hbm, gw), (feat_hbm, feat), (ld_hbm, ld_ref), (k_hbm, k_ref),
            (q_hbm, q_ref), (v_hbm, v_ref), (ridge_hbm, ridge_ref),
        ]
    ):
        c = pltpu.make_async_copy(src, dst, in_sem.at[i])
        c.start()
        loads.append(c)
    loads[0].wait()
    loads[1].wait()
    partial = nt(gw[...], feat[...])
    for j in range(nh):
        gsend[j] = partial[heads * j : heads * (j + 1)]

    pl.semaphore_wait(barrier, nh - 1 + len(near) + ny - 1)

    spans = [r for r in (2, 4, 8, 16) if r < nz // 2]
    if spans:
        signal(ready.at[0], at_z(spans[0]))
        signal(ready.at[0], at_z(-spans[0]))
    gate_copies = []
    for d in range(1, nh):
        to = (me_h + d) % nh
        gate_copies.append(
            send(gsend.at[to], grecv.at[me_h], gs_sem.at[d], gr_sem.at[d], {"head": to})
        )
    grecv[me_h] = gsend[me_h]

    loads[2].wait()
    within = jnp.concatenate([ld_ref[...]] * (8 // heads), axis=0)
    place = lax.broadcasted_iota(jnp.int32, (8, rows), 1) % BLOCK
    step = 1
    while step < BLOCK:
        within = within + jnp.where(place >= step, pltpu.roll(within, step, 1), 0.0)
        step *= 2
    loads[3].wait()
    ksq = []
    for h in range(heads):
        kf = k_ref[:, h * width : (h + 1) * width].astype(F32)
        ksq.append(column_sums(kf * kf)[0:1])
    knorm = jnp.sqrt(jnp.concatenate(ksq, axis=0) + 1e-06)
    kinv = 1.0 / knorm
    within = within[0:heads]
    ends = [within[:, (b + 1) * BLOCK - 1 : (b + 1) * BLOCK] for b in range(blocks)]
    total_row = jnp.concatenate([jnp.broadcast_to(e, (heads, BLOCK)) for e in ends], axis=1)
    tail = jnp.exp(total_row - within)
    ltot = functools.reduce(lambda a, b: a + b, ends)
    both_rows = jnp.concatenate([within, jnp.exp(within)], axis=0)
    cols = jnp.transpose(jnp.concatenate([both_rows] * (128 // (2 * heads)), axis=0))

    def col(kind, h, b):
        return cols[b * BLOCK : (b + 1) * BLOCK, kind * heads + h : kind * heads + h + 1]

    for h in range(heads):
        kt_ref[h] = jnp.transpose(k_ref[:, h * width : (h + 1) * width].astype(F32))

    for turn in range(1, len(spans)):
        pl.semaphore_wait(ready.at[turn - 1], 2)
        signal(ready.at[turn], at_z(spans[turn]))
        signal(ready.at[turn], at_z(-spans[turn]))

    loads[5].wait()
    for c in gate_copies:
        c.wait()
    logits = grecv[0]
    for j in range(1, nh):
        logits = logits + grecv[j]
    beta = 1.0 / (1.0 + jnp.exp(-logits))
    vfac = tail * beta * kinv
    kfac = vfac * kinv

    def keys(h, b):
        return k_ref[b * BLOCK : (b + 1) * BLOCK, h * width : (h + 1) * width]

    def values(h, b):
        return v_ref[b * BLOCK : (b + 1) * BLOCK, h * width : (h + 1) * width]

    order = sorted(range(1, nz), key=lambda d: -min(d, nz - d))
    lane_row = lax.broadcasted_iota(jnp.int32, (1, width), 1)
    sends = []

    def state_update(h, factor, right):
        ups = []
        for b in range(blocks):
            sl = slice(b * BLOCK, (b + 1) * BLOCK)
            hi, lo = split(kt_ref[h, :, sl] * factor[h : h + 1, sl])
            prod = nn(jnp.concatenate([hi, lo], axis=0), right(h, b))
            ups.append(prod[:width] + prod[width:])
        total = ups[0]
        for b in range(1, blocks):
            total = total * jnp.exp(ends[b][h : h + 1]) + ups[b]
        return ups, total

    def hand_in(piece):
        out = []
        for d in order:
            to = (me_z + d) % nz
            out.append(
                send(
                    sbuf.at[piece, to, pl.ds(0, counts[piece])],
                    rbuf.at[piece, me_z, pl.ds(0, counts[piece])],
                    ss_sem.at[piece, d], sr_sem.at[piece, d], at_z(d),
                )
            )
        sends.append(out)
        rbuf[piece, me_z] = sbuf[piece, me_z]

    kk_ups, vk_ups = [], []
    for h in range(heads):
        ups, total = state_update(h, kfac, keys)
        kk_ups.append(ups)
        folded, diagonal = pack(total, width)
        last = jnp.where(lane_row < width // 2, diagonal, ltot[h : h + 1])
        for c in range(nz):
            sbuf[0, c, h * fold : (h + 1) * fold] = folded[c * fold : (c + 1) * fold]
            sbuf[0, c, heads * fold + h : heads * fold + h + 1] = last
    if spans:
        pl.semaphore_wait(ready.at[len(spans) - 1], 2)
    hand_in(0)
    for h in range(heads):
        ups, total = state_update(h, vfac, values)
        vk_ups.append(ups)
        for c in range(nz):
            sbuf[1, c, h * part : (h + 1) * part] = total[c * part : (c + 1) * part]
    hand_in(1)

    lower = lax.broadcasted_iota(jnp.int32, (BLOCK, BLOCK), 0) >= lax.broadcasted_iota(
        jnp.int32, (BLOCK, BLOCK), 1
    )
    loads[4].wait()
    loads[6].wait()
    qunit, qinv = [], []
    for h in range(heads):
        qf = q_ref[:, h * width : (h + 1) * width].astype(F32)
        root = jnp.sqrt(jnp.sum(qf * qf, axis=-1, keepdims=True) + 1e-06)
        qunit.append(qf / root)
        qinv.append(1.0 / root)
    row1 = beta * kinv * kinv
    row2 = beta * kinv

    def prepare(h):
        for b in range(blocks):
            i = h * blocks + b
            sl = slice(b * BLOCK, (b + 1) * BLOCK)
            spread = col(0, h, b) - within[h : h + 1, sl]
            decay = jnp.where(lower, jnp.exp(jnp.minimum(spread, 0.0)), 0.0)
            w1 = decay * row1[h : h + 1, sl]
            w1_ref[i] = w1
            w2_ref[i] = decay * row2[h : h + 1, sl]
            kb = keys(h, b)
            s = nt(q_ref[sl, h * width : (h + 1) * width], kb) * qinv[h][sl]
            s1_ref[i] = s
            hi, lo = split(s * w1)
            in1_ref[i] = nn(hi, kb) + nn(lo, kb)

    def row_gain(piece, logs):
        row = lax.broadcasted_iota(jnp.int32, (counts[piece], 1), 0)
        own = row >= part if piece else ((row >= fold) & (row < heads * fold)) | (row > heads * fold)
        return jnp.exp(jnp.where(own, logs[1], logs[0]))

    def logs_of(chunk):
        return [chunk[heads * fold + h : heads * fold + h + 1, width - 1 : width] for h in range(heads)]

    def y_copy(piece, source, target):
        return pltpu.make_async_remote_copy(
            src_ref=ybuf.at[piece, pl.ds(0, counts[piece])],
            dst_ref=yrecv.at[piece, source, pl.ds(0, counts[piece])],
            send_sem=ys_sem.at[piece, target], recv_sem=yr_sem.at[piece, source],
            device_id={"seq": target * nz + me_z}, device_id_type=MESH,
        )

    def row_prefix(piece):
        for c in sends[piece]:
            c.wait()
        n = counts[piece]
        state = jnp.zeros((n, width), F32)
        gone = [jnp.zeros((1, 1), F32)] * heads
        before = []
        for z in range(nz):
            tbuf[piece, z, 0:n] = state
            before.append(gone)
            logs = logs_of(rbuf[0, z, 0 : counts[0]])
            state = row_gain(piece, logs) * state + rbuf[piece, z, 0:n]
            gone = [g + w for g, w in zip(gone, logs)]
        ybuf[piece, 0:n] = state
        if piece == 0:
            for h in range(heads):
                r = heads * fold + h
                ybuf[0, r : r + 1] = jnp.where(lane_row < width // 2, state[r : r + 1], gone[h])
        for y in range(1, ny):

            @pl.when(me_y < y)
            def _():
                y_copy(piece, me_y, y).start()

        return before

    def give_back(piece, before):
        n = counts[piece]
        carry_ref[piece] = jnp.zeros(carry_ref.shape[1:], F32)
        for y in range(ny - 1):

            @pl.when(y < me_y)
            def _():
                y_copy(piece, y, me_y).wait_recv()
                gain = row_gain(piece, logs_of(yrecv[0, y, 0 : counts[0]]))
                carry_ref[piece, 0:n] = gain * carry_ref[piece, 0:n] + yrecv[piece, y, 0:n]

        carry = carry_ref[piece, 0:n]
        for z in range(nz):
            tbuf[piece, z, 0:n] = tbuf[piece, z, 0:n] + row_gain(piece, before[z]) * carry
        trecv[piece, me_z] = tbuf[piece, me_z]

    def t_copy(piece, to):
        d = (to - me_z + nz) % nz
        return pltpu.make_async_remote_copy(
            src_ref=tbuf.at[piece, to, pl.ds(0, counts[piece])],
            dst_ref=trecv.at[piece, me_z, pl.ds(0, counts[piece])],
            send_sem=ts_sem.at[piece, d], recv_sem=tr_sem.at[piece, d],
            device_id={"seq": me_y * nz + to}, device_id_type=MESH,
        )

    def hand_out(piece, first, last):
        for to in range(first, last):

            @pl.when(to != me_z)
            def _():
                t_copy(piece, to).start()

    bands = [slice(m, m + BLOCK // 2) for m in range(0, BLOCK, BLOCK // 2)]

    def local(scores, weights, i, tall):
        return jnp.concatenate(
            [
                nn(jnp.concatenate(split(u * weights[i, band, 0 : band.stop]), axis=1), t)
                for u, band, t in zip(scores, bands, tall)
            ],
            axis=0,
        )

    def starts(incoming, ups, h):
        out = [incoming]
        for b in range(1, blocks):
            out.append(out[-1] * jnp.exp(ends[b - 1][h : h + 1]) + ups[h][b - 1])
        return out

    def tall(a):
        hi, lo = split(a)
        return jnp.concatenate([hi, hi, lo], axis=0)

    def wide(a):
        hi, lo = split(a)
        return jnp.concatenate([hi, lo, hi], axis=1)

    def solve(hs):
        runs = []
        for h in hs:
            incoming = unpack(
                jnp.concatenate(
                    [trecv[0, c, h * fold : (h + 1) * fold] for c in range(nz)], axis=0
                ),
                trecv[0, 0, heads * fold + h : heads * fold + h + 1],
                width,
            )
            for b, start in enumerate(starts(incoming, kk_ups, h)):
                sl = slice(b * BLOCK, (b + 1) * BLOCK)
                kb = keys(h, b)
                q = qunit[h][sl]
                runs.append(
                    dict(
                        h=h, b=b, i=h * blocks + b, sl=sl, kk=tall(start), lead=col(1, h, b),
                        k_wide=jnp.concatenate([kb, kb], axis=1), p=q, r=q,
                        k_tall=[jnp.concatenate([kb[: m.stop]] * 2, axis=0) for m in bands],
                        norm=jnp.sum(q * q, axis=-1, keepdims=True), ridge=ridge_ref[h : h + 1],
                    )
                )
        for step in range(CG_STEPS):
            for c in runs:
                if step == 0:
                    h = c["h"]
                    q = q_ref[c["sl"], h * width : (h + 1) * width]
                    got = nn(jnp.concatenate([q, q], axis=1), c["kk"][width:])
                    c["state"] = got * (c["lead"] * qinv[h][c["sl"]])
                    c["s"] = [s1_ref[c["i"], top, 0 : top.stop] for top in bands]
                else:
                    three = wide(c["p"])
                    pair = three[:, : 2 * width]
                    c["s"] = [nt(pair[band], c["k_wide"][: band.stop]) for band in bands]
                    c["state"] = c["lead"] * nn(three, c["kk"])
            for c in runs:
                c["near"] = c["state"] + c["ridge"] * c["p"]
                if step == 0:
                    c["image"] = c["near"] + in1_ref[c["i"]]
                elif step < CG_STEPS - 1:
                    c["image"] = c["near"] + local(c["s"], w1_ref, c["i"], c["k_tall"])
            for c in runs:
                p, s = c["p"], c["s"]
                if step == CG_STEPS - 1:
                    energy = jnp.sum(p * c["near"], axis=-1, keepdims=True) + jnp.concatenate(
                        [
                            jnp.sum(u * (u * w1_ref[c["i"], band, 0 : band.stop]), axis=-1, keepdims=True)
                            for u, band in zip(s, bands)
                        ],
                        axis=0,
                    )
                else:
                    energy = jnp.sum(p * c["image"], axis=-1, keepdims=True)
                alpha = c["norm"] / energy
                c["x"] = alpha * p if step == 0 else c["x"] + alpha * p
                scaled = [alpha[band] * u for u, band in zip(s, bands)]
                c["sum"] = scaled if step == 0 else [u + w for u, w in zip(c["sum"], scaled)]
                if step < CG_STEPS - 1:
                    c["r"] = c["r"] - alpha * c["image"]
                    after = jnp.sum(c["r"] * c["r"], axis=-1, keepdims=True)
                    c["p"] = c["r"] + (after / c["norm"]) * p
                    c["norm"] = after
        return runs

    def read_out(runs):
        for h in range(heads):
            incoming = trecv[1, :, h * part : (h + 1) * part].reshape(width, width)
            for c, start in zip(runs[h * blocks : (h + 1) * blocks], starts(incoming, vk_ups, h)):
                vb = values(h, c["b"])
                v_tall = [jnp.concatenate([vb[: m.stop]] * 2, axis=0) for m in bands]
                mixed = c["lead"] * nn(wide(c["x"]), tall(start)) + local(
                    c["sum"], w2_ref, c["i"], v_tall
                )
                out_ref[c["sl"], h * width : (h + 1) * width] = mixed.astype(BF16)

    def arrived(piece):
        for d in range(1, nz):
            t_copy(piece, (me_z + d) % nz).wait_recv()

    early = nz // 2
    for h in range(heads):
        prepare(h)
    for piece in range(2):
        give_back(piece, row_prefix(piece))
        hand_out(piece, 0, early)
    for piece in range(2):
        hand_out(piece, early, nz)
    arrived(0)
    runs = solve(range(heads))
    arrived(1)
    read_out(runs)
    for piece in range(2):
        for d in range(1, nz):
            t_copy(piece, (me_z + d) % nz).wait_send()
        for y in range(1, ny):

            @pl.when(me_y < y)
            def _():
                y_copy(piece, me_y, y).wait_send()


def body(ny, nz, nh, features, gate_weight, queries, keys, values, log_decay, ridge):
    rows, columns = queries.shape
    heads, width = ridge.shape
    blocks = rows // BLOCK
    part = width // nz
    vmem = pl.BlockSpec(memory_space=pltpu.VMEM)
    pad = -(-(heads * part) // 8) * 8
    dma = pltpu.SemaphoreType.DMA
    ops = (features, gate_weight.T, queries, keys, values, log_decay.T, ridge)
    return pl.pallas_call(
        functools.partial(kernel, ny, nz, nh),
        out_shape=jax.ShapeDtypeStruct((rows, columns), BF16),
        in_specs=[pl.BlockSpec(memory_space=pl.ANY)] * 7,
        out_specs=vmem,
        scratch_shapes=[pltpu.VMEM(o.shape, o.dtype) for o in ops]
        + [
            pltpu.VMEM((nh, heads, rows), F32),
            pltpu.VMEM((nh, heads, rows), F32),
            pltpu.VMEM((2, nz, pad, width), F32),
            pltpu.VMEM((2, nz, pad, width), F32),
            pltpu.VMEM((2, pad, width), F32),
            pltpu.VMEM((2, ny, pad, width), F32),
            pltpu.VMEM((2, pad, width), F32),
            pltpu.VMEM((2, nz, pad, width), F32),
            pltpu.VMEM((2, nz, pad, width), F32),
            pltpu.VMEM((heads, width, rows), F32),
            pltpu.VMEM((heads * blocks, BLOCK, BLOCK), F32),
            pltpu.VMEM((heads * blocks, BLOCK, BLOCK), F32),
            pltpu.VMEM((heads * blocks, BLOCK, BLOCK), F32),
            pltpu.VMEM((heads * blocks, BLOCK, width), F32),
            dma((7,)), pltpu.SemaphoreType.REGULAR((4,)),
            dma((nh,)), dma((nh,)), dma((2, nz)), dma((2, nz)),
            dma((2, ny)), dma((2, ny)), dma((2, nz)), dma((2, nz)),
        ],
        compiler_params=pltpu.CompilerParams(collective_id=0, has_side_effects=True),
        name="mesa",
    )(*ops)


def solution(mesh):
    seq, nh = mesh.shape["seq"], mesh.shape["head"]
    nz = 16 if seq >= 64 else seq // 2
    placed = (
        P("seq", "head"),
        P("head", None),
        P("seq", "head"),
        P("seq", "head"),
        P("seq", "head"),
        P("seq", "head"),
        P("head", None),
    )
    return jax.shard_map(
        functools.partial(body, seq // nz, nz, nh),
        mesh=mesh, in_specs=placed, out_specs=P("seq", "head"), check_vma=False,
    )
```

```python
import functools

import jax
import jax.numpy as jnp
from jax import lax
from jax.experimental import pallas as pl
from jax.experimental.pallas import tpu as pltpu
from jax.sharding import PartitionSpec as P

CG_STEPS = 4
BLOCK = 256
MESH = pl.DeviceIdType.MESH
F32 = jnp.float32
BF16 = jnp.bfloat16


def nn(a, b):
    return jnp.dot(a, b, preferred_element_type=F32)


def nt(a, b):
    return lax.dot_general(a, b, (((1,), (1,)), ((), ())), preferred_element_type=F32)


def tn(a, b):
    return lax.dot_general(a, b, (((0,), (0,)), ((), ())), preferred_element_type=F32)


def split(a):
    hi = a.astype(BF16)
    return hi, (a - hi.astype(F32)).astype(BF16)


def column_sums(sq):
    ones = jnp.ones((8, sq.shape[1]), BF16)
    hi, lo = split(sq)
    return nt(ones, hi) + nt(ones, lo)


def pack(total, width):
    half = width // 2
    lane = lax.broadcasted_iota(jnp.int32, (half, width), 1)
    row = lax.broadcasted_iota(jnp.int32, (half, width), 0)
    top = total[0:half]
    turned = pltpu.roll(total[half:width], half, 1)
    folded = jnp.where(lane >= row, top, turned)
    diagonal = jnp.sum(jnp.where(lane == row, turned, 0.0), axis=0, keepdims=True)
    return folded, diagonal


def unpack(folded, diagonal, width):
    half = width // 2
    lane = lax.broadcasted_iota(jnp.int32, (half, width), 1)
    row = lax.broadcasted_iota(jnp.int32, (half, width), 0)
    flipped = jnp.transpose(jnp.concatenate([folded, jnp.zeros_like(folded)], axis=0))
    top = jnp.where(lane >= row, folded, flipped[0:half])
    corner = jnp.where(lane == row, diagonal, jnp.where(lane < row, folded, flipped[0:half]))
    bottom = jnp.where(lane < half, flipped[half:width], pltpu.roll(corner, half, 1))
    return jnp.concatenate([top, bottom], axis=0)


def kernel(
    ny, nz, nh, feat_hbm, gw_hbm, q_hbm, k_hbm, v_hbm, ld_hbm, ridge_hbm, out_ref,
    feat, gw, q_ref, k_ref, v_ref, ld_ref, ridge_ref,
    gsend, grecv, sbuf, rbuf, ybuf, yrecv, carry_ref, tbuf, trecv, kt_ref, w1_ref, w2_ref, s1_ref, in1_ref,
    in_sem, ready, gs_sem, gr_sem, ss_sem, sr_sem, ys_sem, yr_sem, ts_sem, tr_sem,
):
    rows = q_ref.shape[0]
    heads = ridge_ref.shape[0]
    width = ridge_ref.shape[1]
    blocks = rows // BLOCK
    part = width // nz
    fold = part // 2
    extra = heads * fold
    counts = (extra + 1, heads * part)
    half = width // 2
    log_lane = (half, half + half // heads)
    seq = lax.axis_index("seq")
    me_h = lax.axis_index("head")
    me_y = seq // nz
    me_z = seq % nz

    def at_z(d):
        return {"seq": me_y * nz + (me_z + d + nz) % nz}

    def at_y(d):
        return {"seq": ((me_y + d) % ny) * nz + me_z}

    def signal(sem, where):
        pl.semaphore_signal(sem, inc=1, device_id=where, device_id_type=MESH)

    def send(src, dst, sem_out, sem_in, where):
        c = pltpu.make_async_remote_copy(
            src_ref=src, dst_ref=dst, send_sem=sem_out, recv_sem=sem_in,
            device_id=where, device_id_type=MESH,
        )
        c.start()
        return c

    barrier = pltpu.get_barrier_semaphore()
    for d in range(1, nh):
        signal(barrier, {"head": (me_h + d) % nh})
    near = sorted({d % nz for d in (1, -1, 2, -2)} - {0})
    for d in near:
        signal(barrier, at_z(d))
    for d in range(1, ny):
        signal(barrier, at_y(d))

    loads = []
    for i, (src, dst) in enumerate(
        [
            (gw_hbm, gw), (feat_hbm, feat), (ld_hbm, ld_ref), (k_hbm, k_ref),
            (q_hbm, q_ref), (v_hbm, v_ref), (ridge_hbm, ridge_ref),
        ]
    ):
        loads.append(pltpu.make_async_copy(src, dst, in_sem.at[i]))
    for c in loads[:3]:
        c.start()
    loads[0].wait()
    loads[1].wait()
    for c in loads[3:]:
        c.start()
    partial = nt(gw[...], feat[...])
    for j in range(nh):
        gsend[j] = partial[heads * j : heads * (j + 1)]

    pl.semaphore_wait(barrier, nh - 1 + len(near) + ny - 1)

    spans = [r for r in (2, 4, 8, 16) if r < nz // 2]
    if spans:
        signal(ready.at[0], at_z(spans[0]))
        signal(ready.at[0], at_z(-spans[0]))
    gate_copies = []
    for d in range(1, nh):
        to = (me_h + d) % nh
        gate_copies.append(
            send(gsend.at[to], grecv.at[me_h], gs_sem.at[d], gr_sem.at[d], {"head": to})
        )
    grecv[me_h] = gsend[me_h]

    loads[2].wait()
    within = jnp.concatenate([ld_ref[...]] * (8 // heads), axis=0)
    place = lax.broadcasted_iota(jnp.int32, (8, rows), 1) % BLOCK
    step = 1
    while step < BLOCK:
        within = within + jnp.where(place >= step, pltpu.roll(within, step, 1), 0.0)
        step *= 2
    loads[3].wait()
    ksq = []
    for h in range(heads):
        kf = k_ref[:, h * width : (h + 1) * width].astype(F32)
        ksq.append(column_sums(kf * kf)[0:1])
    knorm = jnp.sqrt(jnp.concatenate(ksq, axis=0) + 1e-06)
    kinv = 1.0 / knorm
    within = within[0:heads]
    ends = [within[:, (b + 1) * BLOCK - 1 : (b + 1) * BLOCK] for b in range(blocks)]
    total_row = jnp.concatenate([jnp.broadcast_to(e, (heads, BLOCK)) for e in ends], axis=1)
    tail = jnp.exp(total_row - within)
    ltot = functools.reduce(lambda a, b: a + b, ends)
    both_rows = jnp.concatenate([within, jnp.exp(within)], axis=0)
    cols = jnp.transpose(jnp.concatenate([both_rows] * (128 // (2 * heads)), axis=0))

    def col(kind, h, b):
        return cols[b * BLOCK : (b + 1) * BLOCK, kind * heads + h : kind * heads + h + 1]

    for h in range(heads):
        kt_ref[h] = jnp.transpose(k_ref[:, h * width : (h + 1) * width].astype(F32))

    for turn in range(1, len(spans)):
        pl.semaphore_wait(ready.at[turn - 1], 2)
        signal(ready.at[turn], at_z(spans[turn]))
        signal(ready.at[turn], at_z(-spans[turn]))

    loads[5].wait()
    for c in gate_copies:
        c.wait()
    logits = grecv[0]
    for j in range(1, nh):
        logits = logits + grecv[j]
    beta = 1.0 / (1.0 + jnp.exp(-logits))
    vfac = tail * beta * kinv
    kfac = vfac * kinv

    def keys(h, b):
        return k_ref[b * BLOCK : (b + 1) * BLOCK, h * width : (h + 1) * width]

    def values(h, b):
        return v_ref[b * BLOCK : (b + 1) * BLOCK, h * width : (h + 1) * width]

    order = sorted(range(1, nz), key=lambda d: -min(d, nz - d))
    lane_row = lax.broadcasted_iota(jnp.int32, (1, width), 1)
    def state_update(h, factor, right):
        ups = []
        for b in range(blocks):
            sl = slice(b * BLOCK, (b + 1) * BLOCK)
            hi, lo = split(kt_ref[h, :, sl] * factor[h : h + 1, sl])
            prod = nn(jnp.concatenate([hi, lo], axis=0), right(h, b))
            ups.append(prod[:width] + prod[width:])
        total = ups[0]
        for b in range(1, blocks):
            total = total * jnp.exp(ends[b][h : h + 1]) + ups[b]
        return ups, total

    def s_copy(piece, d):
        return pltpu.make_async_remote_copy(
            src_ref=sbuf.at[piece, (me_z + d) % nz, pl.ds(0, counts[piece])],
            dst_ref=rbuf.at[piece, me_z, pl.ds(0, counts[piece])],
            send_sem=ss_sem.at[piece, d], recv_sem=sr_sem.at[piece, d],
            device_id=at_z(d), device_id_type=MESH,
        )

    def hand_in(piece):
        for d in order:
            s_copy(piece, d).start()

    def handed_in(piece):
        for d in order:
            s_copy(piece, d).wait_recv()

    kk_ups, vk_ups, diagonals = [], [], []
    for h in range(heads):
        ups, total = state_update(h, kfac, keys)
        kk_ups.append(ups)
        folded, diagonal = pack(total, width)
        diagonals.append(diagonal)
        for c in range(nz):
            sbuf[0, c, h * fold : (h + 1) * fold] = folded[c * fold : (c + 1) * fold]
    logs_row = jnp.where(lane_row < log_lane[1], ltot[0:1], ltot[1:2])
    for c in range(nz):
        sbuf[0, c, extra : extra + 1] = jnp.where(lane_row < half, diagonals[min(c, 1)], logs_row)
    if spans:
        pl.semaphore_wait(ready.at[len(spans) - 1], 2)
    hand_in(0)
    rbuf[0, me_z] = sbuf[0, me_z]
    for h in range(heads):
        ups, total = state_update(h, vfac, values)
        vk_ups.append(ups)
        for c in range(nz):
            sbuf[1, c, h * part : (h + 1) * part] = total[c * part : (c + 1) * part]
    rbuf[1, me_z] = sbuf[1, me_z]

    at_once = me_h % 2 == 0

    @pl.when(at_once)
    def _():
        hand_in(1)

    lower = lax.broadcasted_iota(jnp.int32, (BLOCK, BLOCK), 0) >= lax.broadcasted_iota(
        jnp.int32, (BLOCK, BLOCK), 1
    )
    loads[4].wait()
    loads[6].wait()
    qunit, qinv = [], []
    for h in range(heads):
        qf = q_ref[:, h * width : (h + 1) * width].astype(F32)
        root = jnp.sqrt(jnp.sum(qf * qf, axis=-1, keepdims=True) + 1e-06)
        qunit.append(qf / root)
        qinv.append(1.0 / root)
    row1 = beta * kinv * kinv
    row2 = beta * kinv

    def prepare(h):
        for b in range(blocks):
            i = h * blocks + b
            sl = slice(b * BLOCK, (b + 1) * BLOCK)
            spread = col(0, h, b) - within[h : h + 1, sl]
            decay = jnp.where(lower, jnp.exp(jnp.minimum(spread, 0.0)), 0.0)
            w1 = decay * row1[h : h + 1, sl]
            w1_ref[i] = w1
            w2_ref[i] = decay * row2[h : h + 1, sl]
            kb = keys(h, b)
            s = nt(q_ref[sl, h * width : (h + 1) * width], kb) * qinv[h][sl]
            s1_ref[i] = s
            hi, lo = split(s * w1)
            in1_ref[i] = nn(hi, kb) + nn(lo, kb)

    def row_gain(piece, logs):
        row = lax.broadcasted_iota(jnp.int32, (counts[piece], 1), 0)
        if piece:
            second = row >= part
        else:
            second = (row >= fold) & (row < extra) | (row == extra) & (me_z > 0)
        return jnp.exp(jnp.where(second, logs[1], logs[0]))

    def logs_of(chunk):
        return [chunk[extra : extra + 1, at : at + 1] for at in log_lane]

    def y_copy(piece, source, target):
        return pltpu.make_async_remote_copy(
            src_ref=ybuf.at[piece, pl.ds(0, counts[piece])],
            dst_ref=yrecv.at[piece, source, pl.ds(0, counts[piece])],
            send_sem=ys_sem.at[piece, target], recv_sem=yr_sem.at[piece, source],
            device_id={"seq": target * nz + me_z}, device_id_type=MESH,
        )

    def row_prefix(piece):
        if piece == 1:
            handed_in(1)
        n = counts[piece]
        state = jnp.zeros((n, width), F32)
        gone = [jnp.zeros((1, 1), F32)] * heads
        before = []
        for z in range(nz):
            tbuf[piece, z, 0:n] = state
            before.append(gone)
            logs = logs_of(rbuf[0, z, 0 : counts[0]])
            state = row_gain(piece, logs) * state + rbuf[piece, z, 0:n]
            gone = [g + w for g, w in zip(gone, logs)]
        ybuf[piece, 0:n] = state
        if piece == 0:
            ends_row = jnp.where(lane_row < log_lane[1], gone[0], gone[1])
            ybuf[0, extra : extra + 1] = jnp.where(lane_row < half, state[extra : extra + 1], ends_row)
        for y in range(1, ny):

            @pl.when(me_y < y)
            def _():
                y_copy(piece, me_y, y).start()

        return before

    def give_back(piece):
        n = counts[piece]
        carry_ref[piece] = jnp.zeros(carry_ref.shape[1:], F32)
        for y in range(ny - 1):

            @pl.when(y < me_y)
            def _():
                y_copy(piece, y, me_y).wait_recv()
                gain = row_gain(piece, logs_of(yrecv[0, y, 0 : counts[0]]))
                carry_ref[piece, 0:n] = gain * carry_ref[piece, 0:n] + yrecv[piece, y, 0:n]

    def hand_out(piece, before, first, last):
        n = counts[piece]
        carry = carry_ref[piece, 0:n]
        for z in range(first, last):
            tbuf[piece, z, 0:n] = tbuf[piece, z, 0:n] + row_gain(piece, before[z]) * carry

            @pl.when(z != me_z)
            def _():
                t_copy(piece, z).start()

    def t_copy(piece, to):
        d = (to - me_z + nz) % nz
        return pltpu.make_async_remote_copy(
            src_ref=tbuf.at[piece, to, pl.ds(0, counts[piece])],
            dst_ref=trecv.at[piece, me_z, pl.ds(0, counts[piece])],
            send_sem=ts_sem.at[piece, d], recv_sem=tr_sem.at[piece, d],
            device_id={"seq": me_y * nz + to}, device_id_type=MESH,
        )

    bands = [slice(m, m + BLOCK // 2) for m in range(0, BLOCK, BLOCK // 2)]

    def local(scores, weights, i, tall):
        return jnp.concatenate(
            [
                nn(jnp.concatenate(split(u * weights[i, band, 0 : band.stop]), axis=1), t)
                for u, band, t in zip(scores, bands, tall)
            ],
            axis=0,
        )

    def starts(incoming, ups, h):
        out = [incoming]
        for b in range(1, blocks):
            out.append(out[-1] * jnp.exp(ends[b - 1][h : h + 1]) + ups[h][b - 1])
        return out

    def tall(a):
        hi, lo = split(a)
        return jnp.concatenate([hi, hi, lo], axis=0)

    def wide(a):
        hi, lo = split(a)
        return jnp.concatenate([hi, lo, hi], axis=1)

    def solve(hs):
        runs = []
        for h in hs:
            incoming = unpack(
                jnp.concatenate(
                    [trecv[0, c, h * fold : (h + 1) * fold] for c in range(nz)], axis=0
                ),
                trecv[0, h, extra : extra + 1],
                width,
            )
            for b, start in enumerate(starts(incoming, kk_ups, h)):
                sl = slice(b * BLOCK, (b + 1) * BLOCK)
                kb = keys(h, b)
                q = qunit[h][sl]
                runs.append(
                    dict(
                        h=h, b=b, i=h * blocks + b, sl=sl, kk=tall(start), lead=col(1, h, b),
                        k_wide=jnp.concatenate([kb, kb], axis=1), p=q, r=q,
                        k_tall=[jnp.concatenate([kb[: m.stop]] * 2, axis=0) for m in bands],
                        norm=jnp.sum(q * q, axis=-1, keepdims=True), ridge=ridge_ref[h : h + 1],
                    )
                )
        for step in range(CG_STEPS):
            for c in runs:
                if step == 0:
                    h = c["h"]
                    q = q_ref[c["sl"], h * width : (h + 1) * width]
                    got = nn(jnp.concatenate([q, q], axis=1), c["kk"][width:])
                    c["state"] = got * (c["lead"] * qinv[h][c["sl"]])
                    c["s"] = [s1_ref[c["i"], top, 0 : top.stop] for top in bands]
                else:
                    three = wide(c["p"])
                    pair = three[:, : 2 * width]
                    c["s"] = [nt(pair[band], c["k_wide"][: band.stop]) for band in bands]
                    c["state"] = c["lead"] * nn(three, c["kk"])
            for c in runs:
                c["near"] = c["state"] + c["ridge"] * c["p"]
                if step == 0:
                    c["image"] = c["near"] + in1_ref[c["i"]]
                elif step < CG_STEPS - 1:
                    c["image"] = c["near"] + local(c["s"], w1_ref, c["i"], c["k_tall"])
            for c in runs:
                p, s = c["p"], c["s"]
                if step == CG_STEPS - 1:
                    energy = jnp.sum(p * c["near"], axis=-1, keepdims=True) + jnp.concatenate(
                        [
                            jnp.sum(u * (u * w1_ref[c["i"], band, 0 : band.stop]), axis=-1, keepdims=True)
                            for u, band in zip(s, bands)
                        ],
                        axis=0,
                    )
                else:
                    energy = jnp.sum(p * c["image"], axis=-1, keepdims=True)
                alpha = c["norm"] / energy
                c["x"] = alpha * p if step == 0 else c["x"] + alpha * p
                if step < CG_STEPS - 1:
                    c["r"] = c["r"] - alpha * c["image"]
                    after = jnp.sum(c["r"] * c["r"], axis=-1, keepdims=True)
                    c["p"] = c["r"] + (after / c["norm"]) * p
                    c["norm"] = after
        for c in runs:
            c["x_wide"] = wide(c["x"])
            pair = c["x_wide"][:, : 2 * width]
            x_scores = [nt(pair[band], c["k_wide"][: band.stop]) for band in bands]
            vb = values(c["h"], c["b"])
            v_tall = [jnp.concatenate([vb[: m.stop]] * 2, axis=0) for m in bands]
            c["near"] = local(x_scores, w2_ref, c["i"], v_tall)
        return runs

    def read_out(runs):
        for h in range(heads):
            incoming = trecv[1, :, h * part : (h + 1) * part].reshape(width, width)
            for c, start in zip(runs[h * blocks : (h + 1) * blocks], starts(incoming, vk_ups, h)):
                mixed = c["lead"] * nn(c["x_wide"], tall(start)) + c["near"]
                out_ref[c["sl"], h * width : (h + 1) * width] = mixed.astype(BF16)

    def arrived(piece):
        for d in range(1, nz):
            t_copy(piece, (me_z + d) % nz).wait_recv()

    early = nz // 2
    for h in range(heads):
        prepare(h)
    handed_in(0)

    @pl.when(jnp.logical_not(at_once))
    def _():
        hand_in(1)

    before = []
    for piece in range(2):
        before.append(row_prefix(piece))
        give_back(piece)
        hand_out(piece, before[piece], 0, early)
    for piece in range(2):
        hand_out(piece, before[piece], early, nz)
        trecv[piece, me_z] = tbuf[piece, me_z]
    arrived(0)
    runs = solve(range(heads))
    arrived(1)
    read_out(runs)
    for piece in range(2):
        for d in range(1, nz):
            t_copy(piece, (me_z + d) % nz).wait_send()
            s_copy(piece, d).wait_send()
        for y in range(1, ny):

            @pl.when(me_y < y)
            def _():
                y_copy(piece, me_y, y).wait_send()


def body(ny, nz, nh, features, gate_weight, queries, keys, values, log_decay, ridge):
    rows, columns = queries.shape
    heads, width = ridge.shape
    blocks = rows // BLOCK
    part = width // nz
    vmem = pl.BlockSpec(memory_space=pltpu.VMEM)
    pad = -(-(heads * part) // 8) * 8
    dma = pltpu.SemaphoreType.DMA
    ops = (features, gate_weight.T, queries, keys, values, log_decay.T, ridge)
    return pl.pallas_call(
        functools.partial(kernel, ny, nz, nh),
        out_shape=jax.ShapeDtypeStruct((rows, columns), BF16),
        in_specs=[pl.BlockSpec(memory_space=pl.ANY)] * 7,
        out_specs=vmem,
        scratch_shapes=[pltpu.VMEM(o.shape, o.dtype) for o in ops]
        + [
            pltpu.VMEM((nh, heads, rows), F32),
            pltpu.VMEM((nh, heads, rows), F32),
            pltpu.VMEM((2, nz, pad, width), F32),
            pltpu.VMEM((2, nz, pad, width), F32),
            pltpu.VMEM((2, pad, width), F32),
            pltpu.VMEM((2, ny, pad, width), F32),
            pltpu.VMEM((2, pad, width), F32),
            pltpu.VMEM((2, nz, pad, width), F32),
            pltpu.VMEM((2, nz, pad, width), F32),
            pltpu.VMEM((heads, width, rows), F32),
            pltpu.VMEM((heads * blocks, BLOCK, BLOCK), F32),
            pltpu.VMEM((heads * blocks, BLOCK, BLOCK), F32),
            pltpu.VMEM((heads * blocks, BLOCK, BLOCK), F32),
            pltpu.VMEM((heads * blocks, BLOCK, width), F32),
            dma((7,)), pltpu.SemaphoreType.REGULAR((4,)),
            dma((nh,)), dma((nh,)), dma((2, nz)), dma((2, nz)),
            dma((2, ny)), dma((2, ny)), dma((2, nz)), dma((2, nz)),
        ],
        compiler_params=pltpu.CompilerParams(collective_id=0, has_side_effects=True),
        name="mesa",
    )(*ops)


def solution(mesh):
    seq, nh = mesh.shape["seq"], mesh.shape["head"]
    nz = 16 if seq >= 64 else seq // 2
    placed = (
        P("seq", "head"),
        P("head", None),
        P("seq", "head"),
        P("seq", "head"),
        P("seq", "head"),
        P("seq", "head"),
        P("head", None),
    )
    return jax.shard_map(
        functools.partial(body, seq // nz, nz, nh),
        mesh=mesh, in_specs=placed, out_specs=P("seq", "head"), check_vma=False,
    )
```

```python
import functools

import jax
import jax.numpy as jnp
from jax import lax
from jax.experimental import pallas as pl
from jax.experimental.pallas import tpu as pltpu
from jax.sharding import PartitionSpec as P

CG_STEPS = 4
BLOCK = 256
MESH = pl.DeviceIdType.MESH
F32 = jnp.float32
BF16 = jnp.bfloat16


def nn(a, b):
    return jnp.dot(a, b, preferred_element_type=F32)


def nt(a, b):
    return lax.dot_general(a, b, (((1,), (1,)), ((), ())), preferred_element_type=F32)


def tn(a, b):
    return lax.dot_general(a, b, (((0,), (0,)), ((), ())), preferred_element_type=F32)


def split(a):
    hi = a.astype(BF16)
    return hi, (a - hi.astype(F32)).astype(BF16)


def column_sums(sq):
    ones = jnp.ones((8, sq.shape[1]), BF16)
    hi, lo = split(sq)
    return nt(ones, hi) + nt(ones, lo)


def pack(total, width):
    half = width // 2
    lane = lax.broadcasted_iota(jnp.int32, (half, width), 1)
    row = lax.broadcasted_iota(jnp.int32, (half, width), 0)
    top = total[0:half]
    turned = pltpu.roll(total[half:width], half, 1)
    folded = jnp.where(lane >= row, top, turned)
    diagonal = jnp.sum(jnp.where(lane == row, turned, 0.0), axis=0, keepdims=True)
    return folded, diagonal


def unpack(folded, diagonal, width):
    half = width // 2
    lane = lax.broadcasted_iota(jnp.int32, (half, width), 1)
    row = lax.broadcasted_iota(jnp.int32, (half, width), 0)
    flipped = jnp.transpose(jnp.concatenate([folded, jnp.zeros_like(folded)], axis=0))
    top = jnp.where(lane >= row, folded, flipped[0:half])
    corner = jnp.where(lane == row, diagonal, jnp.where(lane < row, folded, flipped[0:half]))
    bottom = jnp.where(lane < half, flipped[half:width], pltpu.roll(corner, half, 1))
    return jnp.concatenate([top, bottom], axis=0)


def kernel(
    ny, nz, nh, feat_hbm, gw_hbm, q_hbm, k_hbm, v_hbm, ld_hbm, ridge_hbm, out_ref,
    feat, gw, q_ref, k_ref, v_ref, ld_ref, ridge_ref,
    gsend, grecv, sbuf, rbuf, ybuf, yrecv, carry_ref, tbuf, trecv, kt_ref, w1_ref, w2_ref, s1_ref, in1_ref,
    in_sem, ready, gs_sem, gr_sem, ss_sem, sr_sem, ys_sem, yr_sem, ts_sem, tr_sem,
):
    rows = q_ref.shape[0]
    heads = ridge_ref.shape[0]
    width = ridge_ref.shape[1]
    blocks = rows // BLOCK
    part = width // nz
    fold = part // 2
    extra = heads * fold
    counts = (extra + 1, heads * part)
    half = width // 2
    log_lane = (half, half + half // heads)
    seq = lax.axis_index("seq")
    me_h = lax.axis_index("head")
    me_y = seq // nz
    me_z = seq % nz

    def at_z(d):
        return {"seq": me_y * nz + (me_z + d + nz) % nz}

    def at_y(d):
        return {"seq": ((me_y + d) % ny) * nz + me_z}

    def signal(sem, where):
        pl.semaphore_signal(sem, inc=1, device_id=where, device_id_type=MESH)

    def send(src, dst, sem_out, sem_in, where):
        c = pltpu.make_async_remote_copy(
            src_ref=src, dst_ref=dst, send_sem=sem_out, recv_sem=sem_in,
            device_id=where, device_id_type=MESH,
        )
        c.start()
        return c

    barrier = pltpu.get_barrier_semaphore()
    for d in range(1, nh):
        signal(barrier, {"head": (me_h + d) % nh})
    near = sorted({d % nz for d in (1, -1, 2, -2)} - {0})
    for d in near:
        signal(barrier, at_z(d))
    for d in range(1, ny):
        signal(barrier, at_y(d))

    loads = []
    for i, (src, dst) in enumerate(
        [
            (gw_hbm, gw), (feat_hbm, feat), (ld_hbm, ld_ref), (k_hbm, k_ref),
            (q_hbm, q_ref), (v_hbm, v_ref), (ridge_hbm, ridge_ref),
        ]
    ):
        loads.append(pltpu.make_async_copy(src, dst, in_sem.at[i]))
    for c in loads[:3]:
        c.start()
    loads[0].wait()
    loads[1].wait()
    for c in loads[3:]:
        c.start()
    partial = nt(gw[...], feat[...])
    for j in range(nh):
        gsend[j] = partial[heads * j : heads * (j + 1)]

    pl.semaphore_wait(barrier, nh - 1 + len(near) + ny - 1)

    spans = [r for r in (2, 4, 8, 16) if r < nz // 2]
    if spans:
        signal(ready.at[0], at_z(spans[0]))
        signal(ready.at[0], at_z(-spans[0]))
    gate_copies = []
    for d in range(1, nh):
        to = (me_h + d) % nh
        gate_copies.append(
            send(gsend.at[to], grecv.at[me_h], gs_sem.at[d], gr_sem.at[d], {"head": to})
        )
    grecv[me_h] = gsend[me_h]

    loads[2].wait()
    within = jnp.concatenate([ld_ref[...]] * (8 // heads), axis=0)
    place = lax.broadcasted_iota(jnp.int32, (8, rows), 1) % BLOCK
    step = 1
    while step < BLOCK:
        within = within + jnp.where(place >= step, pltpu.roll(within, step, 1), 0.0)
        step *= 2
    loads[3].wait()
    ksq = []
    for h in range(heads):
        kf = k_ref[:, h * width : (h + 1) * width].astype(F32)
        ksq.append(column_sums(kf * kf)[0:1])
    knorm = jnp.sqrt(jnp.concatenate(ksq, axis=0) + 1e-06)
    kinv = 1.0 / knorm
    within = within[0:heads]
    ends = [within[:, (b + 1) * BLOCK - 1 : (b + 1) * BLOCK] for b in range(blocks)]
    total_row = jnp.concatenate([jnp.broadcast_to(e, (heads, BLOCK)) for e in ends], axis=1)
    tail = jnp.exp(total_row - within)
    ltot = functools.reduce(lambda a, b: a + b, ends)
    both_rows = jnp.concatenate([within, jnp.exp(within)], axis=0)
    cols = jnp.transpose(jnp.concatenate([both_rows] * (128 // (2 * heads)), axis=0))

    def col(kind, h, b):
        return cols[b * BLOCK : (b + 1) * BLOCK, kind * heads + h : kind * heads + h + 1]

    for h in range(heads):
        kt_ref[h] = jnp.transpose(k_ref[:, h * width : (h + 1) * width].astype(F32))

    for turn in range(1, len(spans)):
        pl.semaphore_wait(ready.at[turn - 1], 2)
        signal(ready.at[turn], at_z(spans[turn]))
        signal(ready.at[turn], at_z(-spans[turn]))

    loads[5].wait()
    for c in gate_copies:
        c.wait()
    logits = grecv[0]
    for j in range(1, nh):
        logits = logits + grecv[j]
    beta = 1.0 / (1.0 + jnp.exp(-logits))
    vfac = tail * beta * kinv
    kfac = vfac * kinv

    def keys(h, b):
        return k_ref[b * BLOCK : (b + 1) * BLOCK, h * width : (h + 1) * width]

    def values(h, b):
        return v_ref[b * BLOCK : (b + 1) * BLOCK, h * width : (h + 1) * width]

    order = sorted(range(1, nz), key=lambda d: -min(d, nz - d))
    lane_row = lax.broadcasted_iota(jnp.int32, (1, width), 1)
    def state_update(h, factor, right):
        ups = []
        for b in range(blocks):
            sl = slice(b * BLOCK, (b + 1) * BLOCK)
            hi, lo = split(kt_ref[h, :, sl] * factor[h : h + 1, sl])
            prod = nn(jnp.concatenate([hi, lo], axis=0), right(h, b))
            ups.append(prod[:width] + prod[width:])
        total = ups[0]
        for b in range(1, blocks):
            total = total * jnp.exp(ends[b][h : h + 1]) + ups[b]
        return ups, total

    def s_copy(piece, d):
        return pltpu.make_async_remote_copy(
            src_ref=sbuf.at[piece, (me_z + d) % nz, pl.ds(0, counts[piece])],
            dst_ref=rbuf.at[piece, me_z, pl.ds(0, counts[piece])],
            send_sem=ss_sem.at[piece, d], recv_sem=sr_sem.at[piece, d],
            device_id=at_z(d), device_id_type=MESH,
        )

    def hand_in(piece):
        for d in order:
            s_copy(piece, d).start()

    def handed_in(piece):
        for d in order:
            s_copy(piece, d).wait_recv()

    kk_ups, vk_ups, diagonals = [], [], []
    for h in range(heads):
        ups, total = state_update(h, kfac, keys)
        kk_ups.append(ups)
        folded, diagonal = pack(total, width)
        diagonals.append(diagonal)
        for c in range(nz):
            sbuf[0, c, h * fold : (h + 1) * fold] = folded[c * fold : (c + 1) * fold]
    logs_row = jnp.where(lane_row < log_lane[1], ltot[0:1], ltot[1:2])
    for c in range(nz):
        sbuf[0, c, extra : extra + 1] = jnp.where(lane_row < half, diagonals[min(c, 1)], logs_row)
    if spans:
        pl.semaphore_wait(ready.at[len(spans) - 1], 2)
    hand_in(0)
    rbuf[0, me_z] = sbuf[0, me_z]
    for h in range(heads):
        ups, total = state_update(h, vfac, values)
        vk_ups.append(ups)
        for c in range(nz):
            sbuf[1, c, h * part : (h + 1) * part] = total[c * part : (c + 1) * part]
    rbuf[1, me_z] = sbuf[1, me_z]

    at_once = me_h % 2 == 0

    @pl.when(at_once)
    def _():
        hand_in(1)

    lower = lax.broadcasted_iota(jnp.int32, (BLOCK, BLOCK), 0) >= lax.broadcasted_iota(
        jnp.int32, (BLOCK, BLOCK), 1
    )
    loads[4].wait()
    loads[6].wait()
    qunit, qinv = [], []
    for h in range(heads):
        qf = q_ref[:, h * width : (h + 1) * width].astype(F32)
        root = jnp.sqrt(jnp.sum(qf * qf, axis=-1, keepdims=True) + 1e-06)
        qunit.append(qf / root)
        qinv.append(1.0 / root)
    row1 = beta * kinv * kinv
    row2 = beta * kinv

    def prepare(h):
        for b in range(blocks):
            i = h * blocks + b
            sl = slice(b * BLOCK, (b + 1) * BLOCK)
            spread = col(0, h, b) - within[h : h + 1, sl]
            decay = jnp.where(lower, jnp.exp(jnp.minimum(spread, 0.0)), 0.0)
            w1 = decay * row1[h : h + 1, sl]
            w1_ref[i] = w1
            w2_ref[i] = decay * row2[h : h + 1, sl]
            kb = keys(h, b)
            s = nt(q_ref[sl, h * width : (h + 1) * width], kb) * qinv[h][sl]
            s1_ref[i] = s
            hi, lo = split(s * w1)
            in1_ref[i] = nn(hi, kb) + nn(lo, kb)

    def row_gain(piece, logs):
        row = lax.broadcasted_iota(jnp.int32, (counts[piece], 1), 0)
        if piece:
            second = row >= part
        else:
            second = (row >= fold) & (row < extra) | (row == extra) & (me_z > 0)
        return jnp.exp(jnp.where(second, logs[1], logs[0]))

    def logs_of(chunk):
        return [chunk[extra : extra + 1, at : at + 1] for at in log_lane]

    def y_copy(piece, source, target):
        return pltpu.make_async_remote_copy(
            src_ref=ybuf.at[piece, pl.ds(0, counts[piece])],
            dst_ref=yrecv.at[piece, source, pl.ds(0, counts[piece])],
            send_sem=ys_sem.at[piece, target], recv_sem=yr_sem.at[piece, source],
            device_id={"seq": target * nz + me_z}, device_id_type=MESH,
        )

    def row_prefix(piece):
        if piece == 1:
            handed_in(1)
        n = counts[piece]
        state = jnp.zeros((n, width), F32)
        gone = [jnp.zeros((1, 1), F32)] * heads
        before = []
        for z in range(nz):
            tbuf[piece, z, 0:n] = state
            before.append(gone)
            logs = logs_of(rbuf[0, z, 0 : counts[0]])
            state = row_gain(piece, logs) * state + rbuf[piece, z, 0:n]
            gone = [g + w for g, w in zip(gone, logs)]
        ybuf[piece, 0:n] = state
        if piece == 0:
            ends_row = jnp.where(lane_row < log_lane[1], gone[0], gone[1])
            ybuf[0, extra : extra + 1] = jnp.where(lane_row < half, state[extra : extra + 1], ends_row)
        for y in range(1, ny):

            @pl.when(me_y < y)
            def _():
                y_copy(piece, me_y, y).start()

        return before

    def give_back(piece):
        n = counts[piece]
        carry_ref[piece] = jnp.zeros(carry_ref.shape[1:], F32)
        for y in range(ny - 1):

            @pl.when(y < me_y)
            def _():
                y_copy(piece, y, me_y).wait_recv()
                gain = row_gain(piece, logs_of(yrecv[0, y, 0 : counts[0]]))
                carry_ref[piece, 0:n] = gain * carry_ref[piece, 0:n] + yrecv[piece, y, 0:n]

    def hand_out(piece, before, first, last):
        n = counts[piece]
        carry = carry_ref[piece, 0:n]
        for z in range(first, last):
            tbuf[piece, z, 0:n] = tbuf[piece, z, 0:n] + row_gain(piece, before[z]) * carry

            @pl.when(z != me_z)
            def _():
                t_copy(piece, z).start()

    def t_copy(piece, to):
        d = (to - me_z + nz) % nz
        return pltpu.make_async_remote_copy(
            src_ref=tbuf.at[piece, to, pl.ds(0, counts[piece])],
            dst_ref=trecv.at[piece, me_z, pl.ds(0, counts[piece])],
            send_sem=ts_sem.at[piece, d], recv_sem=tr_sem.at[piece, d],
            device_id={"seq": me_y * nz + to}, device_id_type=MESH,
        )

    bands = [slice(m, m + BLOCK // 2) for m in range(0, BLOCK, BLOCK // 2)]

    def local(scores, weights, i, tall):
        return jnp.concatenate(
            [
                nn(jnp.concatenate(split(u * weights[i, band, 0 : band.stop]), axis=1), t)
                for u, band, t in zip(scores, bands, tall)
            ],
            axis=0,
        )

    def starts(incoming, ups, h):
        out = [incoming]
        for b in range(1, blocks):
            out.append(out[-1] * jnp.exp(ends[b - 1][h : h + 1]) + ups[h][b - 1])
        return out

    def tall(a):
        hi, lo = split(a)
        return jnp.concatenate([hi, hi, lo], axis=0)

    def wide(a):
        hi, lo = split(a)
        return jnp.concatenate([hi, lo, hi], axis=1)

    def solve(hs):
        runs = []
        for h in hs:
            incoming = unpack(
                jnp.concatenate(
                    [trecv[0, c, h * fold : (h + 1) * fold] for c in range(nz)], axis=0
                ),
                trecv[0, h, extra : extra + 1],
                width,
            )
            for b, start in enumerate(starts(incoming, kk_ups, h)):
                sl = slice(b * BLOCK, (b + 1) * BLOCK)
                kb = keys(h, b)
                q = qunit[h][sl]
                runs.append(
                    dict(
                        h=h, b=b, i=h * blocks + b, sl=sl, kk=tall(start), lead=col(1, h, b),
                        k_wide=jnp.concatenate([kb, kb], axis=1), p=q, r=q,
                        k_tall=[jnp.concatenate([kb[: m.stop]] * 2, axis=0) for m in bands],
                        norm=jnp.sum(q * q, axis=-1, keepdims=True), ridge=ridge_ref[h : h + 1],
                    )
                )
        for step in range(CG_STEPS):
            for c in runs:
                if step == 0:
                    h = c["h"]
                    q = q_ref[c["sl"], h * width : (h + 1) * width]
                    got = nn(jnp.concatenate([q, q], axis=1), c["kk"][width:])
                    c["state"] = got * (c["lead"] * qinv[h][c["sl"]])
                    c["s"] = [s1_ref[c["i"], top, 0 : top.stop] for top in bands]
                else:
                    three = wide(c["p"])
                    pair = three[:, : 2 * width]
                    c["s"] = [nt(pair[band], c["k_wide"][: band.stop]) for band in bands]
                    c["state"] = c["lead"] * nn(three, c["kk"])
            for c in runs:
                c["near"] = c["state"] + c["ridge"] * c["p"]
                if step == 0:
                    c["image"] = c["near"] + in1_ref[c["i"]]
                elif step < CG_STEPS - 1:
                    c["image"] = c["near"] + local(c["s"], w1_ref, c["i"], c["k_tall"])
            for c in runs:
                p, s = c["p"], c["s"]
                if step == CG_STEPS - 1:
                    energy = jnp.sum(p * c["near"], axis=-1, keepdims=True) + jnp.concatenate(
                        [
                            jnp.sum(u * (u * w1_ref[c["i"], band, 0 : band.stop]), axis=-1, keepdims=True)
                            for u, band in zip(s, bands)
                        ],
                        axis=0,
                    )
                else:
                    energy = jnp.sum(p * c["image"], axis=-1, keepdims=True)
                alpha = c["norm"] / energy
                c["x"] = alpha * p if step == 0 else c["x"] + alpha * p
                if step < CG_STEPS - 1:
                    c["r"] = c["r"] - alpha * c["image"]
                    after = jnp.sum(c["r"] * c["r"], axis=-1, keepdims=True)
                    c["p"] = c["r"] + (after / c["norm"]) * p
                    c["norm"] = after
        for c in runs:
            c["x_wide"] = wide(c["x"])
            pair = c["x_wide"][:, : 2 * width]
            x_scores = [nt(pair[band], c["k_wide"][: band.stop]) for band in bands]
            vb = values(c["h"], c["b"])
            v_tall = [jnp.concatenate([vb[: m.stop]] * 2, axis=0) for m in bands]
            c["near"] = local(x_scores, w2_ref, c["i"], v_tall)
        return runs

    def read_out(runs):
        for h in range(heads):
            incoming = trecv[1, :, h * part : (h + 1) * part].reshape(width, width)
            for c, start in zip(runs[h * blocks : (h + 1) * blocks], starts(incoming, vk_ups, h)):
                mixed = c["lead"] * nn(c["x_wide"], tall(start)) + c["near"]
                out_ref[c["sl"], h * width : (h + 1) * width] = mixed.astype(BF16)

    def arrived(piece):
        for d in range(1, nz):
            t_copy(piece, (me_z + d) % nz).wait_recv()

    early = nz // 2
    for h in range(heads):
        prepare(h)
    close = [d for d in order if min(d, nz - d) <= 3]
    for d in close:
        s_copy(0, d).wait_recv()

    @pl.when(jnp.logical_not(at_once))
    def _():
        hand_in(1)

    for d in order:
        if d not in close:
            s_copy(0, d).wait_recv()

    before = []
    for piece in range(2):
        before.append(row_prefix(piece))
        give_back(piece)
        hand_out(piece, before[piece], 0, nz)
        trecv[piece, me_z] = tbuf[piece, me_z]
    arrived(0)
    runs = solve(range(heads))
    arrived(1)
    read_out(runs)
    for piece in range(2):
        for d in range(1, nz):
            t_copy(piece, (me_z + d) % nz).wait_send()
            s_copy(piece, d).wait_send()
        for y in range(1, ny):

            @pl.when(me_y < y)
            def _():
                y_copy(piece, me_y, y).wait_send()


def body(ny, nz, nh, features, gate_weight, queries, keys, values, log_decay, ridge):
    rows, columns = queries.shape
    heads, width = ridge.shape
    blocks = rows // BLOCK
    part = width // nz
    vmem = pl.BlockSpec(memory_space=pltpu.VMEM)
    pad = -(-(heads * part) // 8) * 8
    dma = pltpu.SemaphoreType.DMA
    ops = (features, gate_weight.T, queries, keys, values, log_decay.T, ridge)
    return pl.pallas_call(
        functools.partial(kernel, ny, nz, nh),
        out_shape=jax.ShapeDtypeStruct((rows, columns), BF16),
        in_specs=[pl.BlockSpec(memory_space=pl.ANY)] * 7,
        out_specs=vmem,
        scratch_shapes=[pltpu.VMEM(o.shape, o.dtype) for o in ops]
        + [
            pltpu.VMEM((nh, heads, rows), F32),
            pltpu.VMEM((nh, heads, rows), F32),
            pltpu.VMEM((2, nz, pad, width), F32),
            pltpu.VMEM((2, nz, pad, width), F32),
            pltpu.VMEM((2, pad, width), F32),
            pltpu.VMEM((2, ny, pad, width), F32),
            pltpu.VMEM((2, pad, width), F32),
            pltpu.VMEM((2, nz, pad, width), F32),
            pltpu.VMEM((2, nz, pad, width), F32),
            pltpu.VMEM((heads, width, rows), F32),
            pltpu.VMEM((heads * blocks, BLOCK, BLOCK), F32),
            pltpu.VMEM((heads * blocks, BLOCK, BLOCK), F32),
            pltpu.VMEM((heads * blocks, BLOCK, BLOCK), F32),
            pltpu.VMEM((heads * blocks, BLOCK, width), F32),
            dma((7,)), pltpu.SemaphoreType.REGULAR((4,)),
            dma((nh,)), dma((nh,)), dma((2, nz)), dma((2, nz)),
            dma((2, ny)), dma((2, ny)), dma((2, nz)), dma((2, nz)),
        ],
        compiler_params=pltpu.CompilerParams(collective_id=0, has_side_effects=True),
        name="mesa",
    )(*ops)


def solution(mesh):
    seq, nh = mesh.shape["seq"], mesh.shape["head"]
    nz = 16 if seq >= 64 else seq // 2
    placed = (
        P("seq", "head"),
        P("head", None),
        P("seq", "head"),
        P("seq", "head"),
        P("seq", "head"),
        P("seq", "head"),
        P("head", None),
    )
    return jax.shard_map(
        functools.partial(body, seq // nz, nz, nh),
        mesh=mesh, in_specs=placed, out_specs=P("seq", "head"), check_vma=False,
    )
```

```python
import functools

import jax
import jax.numpy as jnp
from jax import lax
from jax.experimental import pallas as pl
from jax.experimental.pallas import tpu as pltpu
from jax.sharding import PartitionSpec as P

CG_STEPS = 4
BLOCK = 256
MESH = pl.DeviceIdType.MESH
F32 = jnp.float32
BF16 = jnp.bfloat16


def nn(a, b):
    return jnp.dot(a, b, preferred_element_type=F32)


def nt(a, b):
    return lax.dot_general(a, b, (((1,), (1,)), ((), ())), preferred_element_type=F32)


def tn(a, b):
    return lax.dot_general(a, b, (((0,), (0,)), ((), ())), preferred_element_type=F32)


def split(a):
    hi = a.astype(BF16)
    return hi, (a - hi.astype(F32)).astype(BF16)


def column_sums(sq):
    ones = jnp.ones((8, sq.shape[1]), BF16)
    hi, lo = split(sq)
    return nt(ones, hi) + nt(ones, lo)


def pack(total, width):
    half = width // 2
    lane = lax.broadcasted_iota(jnp.int32, (half, width), 1)
    row = lax.broadcasted_iota(jnp.int32, (half, width), 0)
    top = total[0:half]
    turned = pltpu.roll(total[half:width], half, 1)
    folded = jnp.where(lane >= row, top, turned)
    diagonal = jnp.sum(jnp.where(lane == row, turned, 0.0), axis=0, keepdims=True)
    return folded, diagonal


def unpack(folded, diagonal, width):
    half = width // 2
    lane = lax.broadcasted_iota(jnp.int32, (half, width), 1)
    row = lax.broadcasted_iota(jnp.int32, (half, width), 0)
    flipped = jnp.transpose(jnp.concatenate([folded, jnp.zeros_like(folded)], axis=0))
    top = jnp.where(lane >= row, folded, flipped[0:half])
    corner = jnp.where(lane == row, diagonal, jnp.where(lane < row, folded, flipped[0:half]))
    bottom = jnp.where(lane < half, flipped[half:width], pltpu.roll(corner, half, 1))
    return jnp.concatenate([top, bottom], axis=0)


def kernel(
    ny, nz, nh, feat_hbm, gw_hbm, q_hbm, k_hbm, v_hbm, ld_hbm, ridge_hbm, out_ref,
    feat, gw, q_ref, k_ref, v_ref, ld_ref, ridge_ref,
    gsend, grecv, sbuf, rbuf, ybuf, yrecv, carry_ref, tbuf, trecv, kt_ref, w1_ref, w2_ref, s1_ref, in1_ref,
    in_sem, ready, gs_sem, gr_sem, ss_sem, sr_sem, ys_sem, yr_sem, ts_sem, tr_sem,
):
    rows = q_ref.shape[0]
    heads = ridge_ref.shape[0]
    width = ridge_ref.shape[1]
    blocks = rows // BLOCK
    part = width // nz
    fold = part // 2
    extra = heads * fold
    counts = (extra + 1, heads * part)
    half = width // 2
    log_lane = (half, half + half // heads)
    seq = lax.axis_index("seq")
    me_h = lax.axis_index("head")
    me_y = seq // nz
    me_z = seq % nz

    def at_z(d):
        return {"seq": me_y * nz + (me_z + d + nz) % nz}

    def at_y(d):
        return {"seq": ((me_y + d) % ny) * nz + me_z}

    def signal(sem, where):
        pl.semaphore_signal(sem, inc=1, device_id=where, device_id_type=MESH)

    def send(src, dst, sem_out, sem_in, where):
        c = pltpu.make_async_remote_copy(
            src_ref=src, dst_ref=dst, send_sem=sem_out, recv_sem=sem_in,
            device_id=where, device_id_type=MESH,
        )
        c.start()
        return c

    barrier = pltpu.get_barrier_semaphore()
    for d in range(1, nh):
        signal(barrier, {"head": (me_h + d) % nh})
    near = sorted({d % nz for d in (1, -1, 2, -2)} - {0})
    for d in near:
        signal(barrier, at_z(d))
    for d in range(1, ny):
        signal(barrier, at_y(d))

    loads = []
    for i, (src, dst) in enumerate(
        [
            (gw_hbm, gw), (feat_hbm, feat), (ld_hbm, ld_ref), (k_hbm, k_ref),
            (q_hbm, q_ref), (v_hbm, v_ref), (ridge_hbm, ridge_ref),
        ]
    ):
        loads.append(pltpu.make_async_copy(src, dst, in_sem.at[i]))
    for c in loads[:3]:
        c.start()
    loads[0].wait()
    loads[1].wait()
    for c in loads[3:]:
        c.start()
    partial = nt(gw[...], feat[...])
    for j in range(nh):
        gsend[j] = partial[heads * j : heads * (j + 1)]

    pl.semaphore_wait(barrier, nh - 1 + len(near) + ny - 1)

    spans = [r for r in (2, 4, 8, 16) if r < nz // 2]
    if spans:
        signal(ready.at[0], at_z(spans[0]))
        signal(ready.at[0], at_z(-spans[0]))
    gate_copies = []
    for d in range(1, nh):
        to = (me_h + d) % nh
        gate_copies.append(
            send(gsend.at[to], grecv.at[me_h], gs_sem.at[d], gr_sem.at[d], {"head": to})
        )
    grecv[me_h] = gsend[me_h]

    loads[2].wait()
    within = jnp.concatenate([ld_ref[...]] * (8 // heads), axis=0)
    place = lax.broadcasted_iota(jnp.int32, (8, rows), 1) % BLOCK
    step = 1
    while step < BLOCK:
        within = within + jnp.where(place >= step, pltpu.roll(within, step, 1), 0.0)
        step *= 2
    loads[3].wait()
    ksq = []
    for h in range(heads):
        kf = k_ref[:, h * width : (h + 1) * width].astype(F32)
        ksq.append(column_sums(kf * kf)[0:1])
    knorm = jnp.sqrt(jnp.concatenate(ksq, axis=0) + 1e-06)
    kinv = 1.0 / knorm
    within = within[0:heads]
    ends = [within[:, (b + 1) * BLOCK - 1 : (b + 1) * BLOCK] for b in range(blocks)]
    total_row = jnp.concatenate([jnp.broadcast_to(e, (heads, BLOCK)) for e in ends], axis=1)
    tail = jnp.exp(total_row - within)
    ltot = functools.reduce(lambda a, b: a + b, ends)
    both_rows = jnp.concatenate([within, jnp.exp(within)], axis=0)
    cols = jnp.transpose(jnp.concatenate([both_rows] * (128 // (2 * heads)), axis=0))

    def col(kind, h, b):
        return cols[b * BLOCK : (b + 1) * BLOCK, kind * heads + h : kind * heads + h + 1]

    for h in range(heads):
        kt_ref[h] = jnp.transpose(k_ref[:, h * width : (h + 1) * width].astype(F32))

    for turn in range(1, len(spans)):
        pl.semaphore_wait(ready.at[turn - 1], 2)
        signal(ready.at[turn], at_z(spans[turn]))
        signal(ready.at[turn], at_z(-spans[turn]))

    loads[5].wait()
    for c in gate_copies:
        c.wait()
    logits = grecv[0]
    for j in range(1, nh):
        logits = logits + grecv[j]
    beta = 1.0 / (1.0 + jnp.exp(-logits))
    vfac = tail * beta * kinv
    kfac = vfac * kinv

    def keys(h, b):
        return k_ref[b * BLOCK : (b + 1) * BLOCK, h * width : (h + 1) * width]

    def values(h, b):
        return v_ref[b * BLOCK : (b + 1) * BLOCK, h * width : (h + 1) * width]

    order = sorted(range(1, nz), key=lambda d: -min(d, nz - d))
    lane_row = lax.broadcasted_iota(jnp.int32, (1, width), 1)
    def state_update(h, factor, right):
        ups = []
        for b in range(blocks):
            sl = slice(b * BLOCK, (b + 1) * BLOCK)
            hi, lo = split(kt_ref[h, :, sl] * factor[h : h + 1, sl])
            prod = nn(jnp.concatenate([hi, lo], axis=0), right(h, b))
            ups.append(prod[:width] + prod[width:])
        total = ups[0]
        for b in range(1, blocks):
            total = total * jnp.exp(ends[b][h : h + 1]) + ups[b]
        return ups, total

    def s_copy(piece, d):
        return pltpu.make_async_remote_copy(
            src_ref=sbuf.at[piece, (me_z + d) % nz, pl.ds(0, counts[piece])],
            dst_ref=rbuf.at[piece, me_z, pl.ds(0, counts[piece])],
            send_sem=ss_sem.at[piece, d], recv_sem=sr_sem.at[piece, d],
            device_id=at_z(d), device_id_type=MESH,
        )

    def hand_in(piece):
        for d in order:
            s_copy(piece, d).start()

    def handed_in(piece):
        for d in order:
            s_copy(piece, d).wait_recv()

    kk_ups, vk_ups, diagonals = [], [], []
    for h in range(heads):
        ups, total = state_update(h, kfac, keys)
        kk_ups.append(ups)
        folded, diagonal = pack(total, width)
        diagonals.append(diagonal)
        for c in range(nz):
            sbuf[0, c, h * fold : (h + 1) * fold] = folded[c * fold : (c + 1) * fold]
    logs_row = jnp.where(lane_row < log_lane[1], ltot[0:1], ltot[1:2])
    for c in range(nz):
        sbuf[0, c, extra : extra + 1] = jnp.where(lane_row < half, diagonals[min(c, 1)], logs_row)
    if spans:
        pl.semaphore_wait(ready.at[len(spans) - 1], 2)
    hand_in(0)
    rbuf[0, me_z] = sbuf[0, me_z]
    for h in range(heads):
        ups, total = state_update(h, vfac, values)
        vk_ups.append(ups)
        for c in range(nz):
            sbuf[1, c, h * part : (h + 1) * part] = total[c * part : (c + 1) * part]
    rbuf[1, me_z] = sbuf[1, me_z]

    at_once = me_h % 2 == 0


    lower = lax.broadcasted_iota(jnp.int32, (BLOCK, BLOCK), 0) >= lax.broadcasted_iota(
        jnp.int32, (BLOCK, BLOCK), 1
    )
    loads[4].wait()
    loads[6].wait()
    qunit, qinv = [], []
    for h in range(heads):
        qf = q_ref[:, h * width : (h + 1) * width].astype(F32)
        root = jnp.sqrt(jnp.sum(qf * qf, axis=-1, keepdims=True) + 1e-06)
        qunit.append(qf / root)
        qinv.append(1.0 / root)
    row1 = beta * kinv * kinv
    row2 = beta * kinv

    def prepare(h):
        for b in range(blocks):
            i = h * blocks + b
            sl = slice(b * BLOCK, (b + 1) * BLOCK)
            spread = col(0, h, b) - within[h : h + 1, sl]
            decay = jnp.where(lower, jnp.exp(jnp.minimum(spread, 0.0)), 0.0)
            w1 = decay * row1[h : h + 1, sl]
            w1_ref[i] = w1
            w2_ref[i] = decay * row2[h : h + 1, sl]
            kb = keys(h, b)
            s = nt(q_ref[sl, h * width : (h + 1) * width], kb) * qinv[h][sl]
            s1_ref[i] = s
            hi, lo = split(s * w1)
            in1_ref[i] = nn(hi, kb) + nn(lo, kb)

    def row_gain(piece, logs):
        row = lax.broadcasted_iota(jnp.int32, (counts[piece], 1), 0)
        if piece:
            second = row >= part
        else:
            second = (row >= fold) & (row < extra) | (row == extra) & (me_z > 0)
        return jnp.exp(jnp.where(second, logs[1], logs[0]))

    def logs_of(chunk):
        return [chunk[extra : extra + 1, at : at + 1] for at in log_lane]

    def y_copy(piece, source, target):
        return pltpu.make_async_remote_copy(
            src_ref=ybuf.at[piece, pl.ds(0, counts[piece])],
            dst_ref=yrecv.at[piece, source, pl.ds(0, counts[piece])],
            send_sem=ys_sem.at[piece, target], recv_sem=yr_sem.at[piece, source],
            device_id={"seq": target * nz + me_z}, device_id_type=MESH,
        )

    def row_prefix(piece):
        if piece == 1:
            handed_in(1)
        n = counts[piece]
        state = jnp.zeros((n, width), F32)
        gone = [jnp.zeros((1, 1), F32)] * heads
        before = []
        for z in range(nz):
            tbuf[piece, z, 0:n] = state
            before.append(gone)
            logs = logs_of(rbuf[0, z, 0 : counts[0]])
            state = row_gain(piece, logs) * state + rbuf[piece, z, 0:n]
            gone = [g + w for g, w in zip(gone, logs)]
        ybuf[piece, 0:n] = state
        if piece == 0:
            ends_row = jnp.where(lane_row < log_lane[1], gone[0], gone[1])
            ybuf[0, extra : extra + 1] = jnp.where(lane_row < half, state[extra : extra + 1], ends_row)
        for y in range(1, ny):

            @pl.when(me_y < y)
            def _():
                y_copy(piece, me_y, y).start()

        return before

    def give_back(piece):
        n = counts[piece]
        carry_ref[piece] = jnp.zeros(carry_ref.shape[1:], F32)
        for y in range(ny - 1):

            @pl.when(y < me_y)
            def _():
                y_copy(piece, y, me_y).wait_recv()
                gain = row_gain(piece, logs_of(yrecv[0, y, 0 : counts[0]]))
                carry_ref[piece, 0:n] = gain * carry_ref[piece, 0:n] + yrecv[piece, y, 0:n]

    def hand_out(piece, before, first, last):
        n = counts[piece]
        carry = carry_ref[piece, 0:n]
        for z in range(first, last):
            tbuf[piece, z, 0:n] = tbuf[piece, z, 0:n] + row_gain(piece, before[z]) * carry

            @pl.when(z != me_z)
            def _():
                t_copy(piece, z).start()

    def t_copy(piece, to):
        d = (to - me_z + nz) % nz
        return pltpu.make_async_remote_copy(
            src_ref=tbuf.at[piece, to, pl.ds(0, counts[piece])],
            dst_ref=trecv.at[piece, me_z, pl.ds(0, counts[piece])],
            send_sem=ts_sem.at[piece, d], recv_sem=tr_sem.at[piece, d],
            device_id={"seq": me_y * nz + to}, device_id_type=MESH,
        )

    bands = [slice(m, m + BLOCK // 2) for m in range(0, BLOCK, BLOCK // 2)]

    def local(scores, weights, i, tall):
        return jnp.concatenate(
            [
                nn(jnp.concatenate(split(u * weights[i, band, 0 : band.stop]), axis=1), t)
                for u, band, t in zip(scores, bands, tall)
            ],
            axis=0,
        )

    def starts(incoming, ups, h):
        out = [incoming]
        for b in range(1, blocks):
            out.append(out[-1] * jnp.exp(ends[b - 1][h : h + 1]) + ups[h][b - 1])
        return out

    def tall(a):
        hi, lo = split(a)
        return jnp.concatenate([hi, hi, lo], axis=0)

    def wide(a):
        hi, lo = split(a)
        return jnp.concatenate([hi, lo, hi], axis=1)

    def solve(hs):
        runs = []
        for h in hs:
            incoming = unpack(
                jnp.concatenate(
                    [trecv[0, c, h * fold : (h + 1) * fold] for c in range(nz)], axis=0
                ),
                trecv[0, h, extra : extra + 1],
                width,
            )
            for b, start in enumerate(starts(incoming, kk_ups, h)):
                sl = slice(b * BLOCK, (b + 1) * BLOCK)
                kb = keys(h, b)
                q = qunit[h][sl]
                runs.append(
                    dict(
                        h=h, b=b, i=h * blocks + b, sl=sl, kk=tall(start), lead=col(1, h, b),
                        k_wide=jnp.concatenate([kb, kb], axis=1), p=q, r=q,
                        k_tall=[jnp.concatenate([kb[: m.stop]] * 2, axis=0) for m in bands],
                        norm=jnp.sum(q * q, axis=-1, keepdims=True), ridge=ridge_ref[h : h + 1],
                    )
                )
        for step in range(CG_STEPS):
            for c in runs:
                if step == 0:
                    h = c["h"]
                    q = q_ref[c["sl"], h * width : (h + 1) * width]
                    got = nn(jnp.concatenate([q, q], axis=1), c["kk"][width:])
                    c["state"] = got * (c["lead"] * qinv[h][c["sl"]])
                    c["s"] = [s1_ref[c["i"], top, 0 : top.stop] for top in bands]
                else:
                    three = wide(c["p"])
                    pair = three[:, : 2 * width]
                    c["s"] = [nt(pair[band], c["k_wide"][: band.stop]) for band in bands]
                    c["state"] = c["lead"] * nn(three, c["kk"])
            for c in runs:
                c["near"] = c["state"] + c["ridge"] * c["p"]
                if step == 0:
                    c["image"] = c["near"] + in1_ref[c["i"]]
                elif step < CG_STEPS - 1:
                    c["image"] = c["near"] + local(c["s"], w1_ref, c["i"], c["k_tall"])
            for c in runs:
                p, s = c["p"], c["s"]
                if step == CG_STEPS - 1:
                    energy = jnp.sum(p * c["near"], axis=-1, keepdims=True) + jnp.concatenate(
                        [
                            jnp.sum(u * (u * w1_ref[c["i"], band, 0 : band.stop]), axis=-1, keepdims=True)
                            for u, band in zip(s, bands)
                        ],
                        axis=0,
                    )
                else:
                    energy = jnp.sum(p * c["image"], axis=-1, keepdims=True)
                alpha = c["norm"] / energy
                c["x"] = alpha * p if step == 0 else c["x"] + alpha * p
                if step < CG_STEPS - 1:
                    c["r"] = c["r"] - alpha * c["image"]
                    after = jnp.sum(c["r"] * c["r"], axis=-1, keepdims=True)
                    c["p"] = c["r"] + (after / c["norm"]) * p
                    c["norm"] = after
        for c in runs:
            c["x_wide"] = wide(c["x"])
            pair = c["x_wide"][:, : 2 * width]
            x_scores = [nt(pair[band], c["k_wide"][: band.stop]) for band in bands]
            vb = values(c["h"], c["b"])
            v_tall = [jnp.concatenate([vb[: m.stop]] * 2, axis=0) for m in bands]
            c["near"] = local(x_scores, w2_ref, c["i"], v_tall)
        return runs

    def read_out(runs):
        for h in range(heads):
            incoming = trecv[1, :, h * part : (h + 1) * part].reshape(width, width)
            for c, start in zip(runs[h * blocks : (h + 1) * blocks], starts(incoming, vk_ups, h)):
                mixed = c["lead"] * nn(c["x_wide"], tall(start)) + c["near"]
                out_ref[c["sl"], h * width : (h + 1) * width] = mixed.astype(BF16)

    def arrived(piece):
        for d in range(1, nz):
            t_copy(piece, (me_z + d) % nz).wait_recv()

    early = nz // 2
    for h in range(heads):
        prepare(h)

    @pl.when(at_once)
    def _():
        hand_in(1)
    close = [d for d in order if min(d, nz - d) <= 3]
    for d in close:
        s_copy(0, d).wait_recv()

    @pl.when(jnp.logical_not(at_once))
    def _():
        hand_in(1)

    for d in order:
        if d not in close:
            s_copy(0, d).wait_recv()

    before = []
    for piece in range(2):
        before.append(row_prefix(piece))
        give_back(piece)
        hand_out(piece, before[piece], 0, nz)
        trecv[piece, me_z] = tbuf[piece, me_z]
    arrived(0)
    runs = solve(range(heads))
    arrived(1)
    read_out(runs)
    for piece in range(2):
        for d in range(1, nz):
            t_copy(piece, (me_z + d) % nz).wait_send()
            s_copy(piece, d).wait_send()
        for y in range(1, ny):

            @pl.when(me_y < y)
            def _():
                y_copy(piece, me_y, y).wait_send()


def body(ny, nz, nh, features, gate_weight, queries, keys, values, log_decay, ridge):
    rows, columns = queries.shape
    heads, width = ridge.shape
    blocks = rows // BLOCK
    part = width // nz
    vmem = pl.BlockSpec(memory_space=pltpu.VMEM)
    pad = -(-(heads * part) // 8) * 8
    dma = pltpu.SemaphoreType.DMA
    ops = (features, gate_weight.T, queries, keys, values, log_decay.T, ridge)
    return pl.pallas_call(
        functools.partial(kernel, ny, nz, nh),
        out_shape=jax.ShapeDtypeStruct((rows, columns), BF16),
        in_specs=[pl.BlockSpec(memory_space=pl.ANY)] * 7,
        out_specs=vmem,
        scratch_shapes=[pltpu.VMEM(o.shape, o.dtype) for o in ops]
        + [
            pltpu.VMEM((nh, heads, rows), F32),
            pltpu.VMEM((nh, heads, rows), F32),
            pltpu.VMEM((2, nz, pad, width), F32),
            pltpu.VMEM((2, nz, pad, width), F32),
            pltpu.VMEM((2, pad, width), F32),
            pltpu.VMEM((2, ny, pad, width), F32),
            pltpu.VMEM((2, pad, width), F32),
            pltpu.VMEM((2, nz, pad, width), F32),
            pltpu.VMEM((2, nz, pad, width), F32),
            pltpu.VMEM((heads, width, rows), F32),
            pltpu.VMEM((heads * blocks, BLOCK, BLOCK), F32),
            pltpu.VMEM((heads * blocks, BLOCK, BLOCK), F32),
            pltpu.VMEM((heads * blocks, BLOCK, BLOCK), F32),
            pltpu.VMEM((heads * blocks, BLOCK, width), F32),
            dma((7,)), pltpu.SemaphoreType.REGULAR((4,)),
            dma((nh,)), dma((nh,)), dma((2, nz)), dma((2, nz)),
            dma((2, ny)), dma((2, ny)), dma((2, nz)), dma((2, nz)),
        ],
        compiler_params=pltpu.CompilerParams(collective_id=0, has_side_effects=True),
        name="mesa",
    )(*ops)


def solution(mesh):
    seq, nh = mesh.shape["seq"], mesh.shape["head"]
    nz = 16 if seq >= 64 else seq // 2
    placed = (
        P("seq", "head"),
        P("head", None),
        P("seq", "head"),
        P("seq", "head"),
        P("seq", "head"),
        P("seq", "head"),
        P("head", None),
    )
    return jax.shard_map(
        functools.partial(body, seq // nz, nz, nh),
        mesh=mesh, in_specs=placed, out_specs=P("seq", "head"), check_vma=False,
    )
```
